32 devices in a mesh: groups: 2 (over y), dp: 4 (over z), section: 2 (over x), tensor: 2 (over core).
Axes of the slice: x: 2, y: 2, z: 4, core: 2. Of those that a mesh axis runs over, the one named last changes fastest.
Arguments:
- cotangent: bfloat16 [2, 1024, 2048], P('section', ('groups', 'dp')), parts along dimension 1, may hold values from -6 to 6
- routes: int32 [2, 8, 2], P('section', ('groups', 'dp')), parts along dimension 1, may hold values from 0 to 3, all different within a row
- gate_values: float32 [2, 1024, 2], P('section', ('groups', 'dp')), parts along dimension 1, may hold values from 0.1 to 0.9
- up_weight: bfloat16 [2, 4, 2048, 7168], P('section', 'dp', None, 'tensor'), may hold values from -0.125 to 0.125
- down_weight: bfloat16 [2, 4, 7168, 2048], P('section', 'dp', 'tensor'), may hold values from -0.0625 to 0.0625
- pre_activation: bfloat16 [2, 8, 4, 128, 7168], P('section', ('groups', 'dp'), None, None, 'tensor'), parts along dimension 1, may hold values from -6 to 6
- input_sketch: float32 [2, 1024, 64], P('section', ('groups', 'dp')), parts along dimension 1, may hold values from -6 to 6
- model_sketch: bfloat16 [2, 2048, 64], P('section'), may hold values from -0.125 to 0.125
- hidden_sketch: bfloat16 [2, 4, 7168, 64], P('section', 'dp', 'tensor'), may hold values from -0.0625 to 0.0625
- lengths: int32 [2, 8, 4], P('section', ('groups', 'dp')), parts along dimension 1, may hold values from 1 to 64, 128 in all within a row
Outputs:
- handed: bfloat16 [2, 1024, 2048], P('section', ('groups', 'dp')), parts along dimension 1
- features: float32 [2, 32, 64, 128], P('section', ('groups', 'dp')), parts along dimension 1
The draws below stay inside these ranges and needn't reach their ends.
There are 2 independent parts, one for each index of `groups`. The reference program is written for one: setup_inputs(seed, part) draws one part's arguments, and reference() takes and returns one part's arrays. A program takes and returns all parts, laid end to end along the dimension named above; an argument that names none is the same for every part. Nothing has to cross between parts.
Inputs may be any that keep to these rules, and one draw needn't show every extreme that they name: `routes`: the two experts of a block differ. `lengths`: each row of counts sums to 128, and its largest is 64.
All inputs are finite; a program needn't handle non-finite values.
Results may differ from the reference program's by a relative error of at most 0.0037.
Values may be sent and summed in bfloat16 or wider, within the bound.
A program may use at most 128 MiB of HBM per device.

```python
import math
import jax
import jax.numpy as jnp
import numpy as np
from jax import lax

D = 2048
FF = 7168
EXPERTS = 4
RANK = 64
BLOCK = 128
TOK_DEV = 128
EX_DEV = 4
MOST_EX = 64
PIECES = 4
FF_PIECE = 7168
TOKENS = 512
BLOCKS = 4
EXAMPLES = 16
SECTIONS = 2


def level_of(own_key, dims, pieces, low, high):
    def one(axis_at, shards_of):
        draws = jax.random.uniform(jax.random.fold_in(jax.random.fold_in(own_key, 6), axis_at), (shards_of,), jnp.float32, low / len(pieces), high / len(pieces))
        return jnp.repeat(jnp.exp(draws), dims[axis_at] // shards_of).reshape((-1,) + (1,) * (len(dims) - axis_at - 1))

    level = one(*pieces[0])
    for cut in pieces[1:]:
        level = level * one(*cut)
    return level


def different_ones(own_key, rows, number_of, top, lift):
    order = jax.random.permutation(jax.random.fold_in(own_key, 1), number_of)
    pull = order
    for power in range(3):
        pull = pull * pull // number_of
    pull = pull * lift // number_of
    lots = jax.random.randint(jax.random.fold_in(own_key, 2), (rows, number_of), 0, 4096) + pull
    fixed_rows = jax.random.permutation(jax.random.fold_in(own_key, 3), rows)[jnp.arange(number_of) % rows]
    lots = jnp.where(jnp.arange(rows)[:, None] == fixed_rows[None, :], 1 << 14, lots)
    score = lots * number_of + jnp.arange(number_of)
    return lax.top_k(score.astype(jnp.int32), top)[1].astype(jnp.int32)


def profile(number_of, total, most, lean):
    loads = [(1 << 20) // math.isqrt(grade ** lean) + 1 for grade in range(2, number_of + 1)]
    spare, given = total - most - (number_of - 1), [1] * (number_of - 1)
    while spare > 0:
        candidates = [i for i in range(number_of - 1) if given[i] < most]
        whole, remaining = sum([loads[i] for i in candidates]), spare
        for i in candidates:
            more = min(most - given[i], max(1, remaining * loads[i] // whole), spare)
            given[i] = given[i] + more
            spare = spare - more
    return np.array([most] + given)


def ragged_sizes(key, count, total, most, lean):
    if count == 2:
        one = jax.random.randint(key, (), max(1, total - most), min(most, total - 1) + 1)
        return jnp.stack([one, total - one])
    sizes = jnp.asarray(profile(count, total, most, lean), jnp.int32)
    pairs = (count - 1) // 2
    source_of, receiver = sizes[1:1 + 2 * pairs:2], sizes[2:2 + 2 * pairs:2]
    margin = jnp.minimum(source_of - 1, most - receiver)
    moved = jax.random.randint(jax.random.fold_in(key, 1), (pairs,), 0, 1 << 20) % (margin + 1)
    sizes = sizes.at[1:1 + 2 * pairs:2].set(source_of - moved).at[2:2 + 2 * pairs:2].set(receiver + moved)
    return sizes[jax.random.permutation(jax.random.fold_in(key, 2), count)]


def noise(stream_key, extent, width, limit, pieces=(), kind=jnp.bfloat16):
    result = jax.random.normal(stream_key, extent, jnp.float32) * width
    if len(pieces) > 0:
        result = level_of(stream_key, extent, pieces, -0.22, 0.18) * result
    return jnp.clip(result, min=-limit, max=limit).astype(kind)


def setup_inputs(seed: int = 0, part: int = 0) -> dict:
    key_of = jax.random.split(jax.random.key(seed), 11)
    own_keys = jax.random.split(jax.random.fold_in(key_of[10], part), 11)
    cotangent = noise(own_keys[0], (SECTIONS, TOKENS, D), 1.0, 6.0, ((0, 2), (1, 4)))
    routes = different_ones(own_keys[1], SECTIONS * BLOCKS, EXPERTS, 2, 8192).reshape((SECTIONS, BLOCKS, 2))
    gate_values = jnp.clip(0.1 + 0.79999997 * jax.random.uniform(own_keys[2], (SECTIONS, TOKENS, 2), jnp.float32) ** level_of(own_keys[2], (SECTIONS, TOKENS, 2), ((0, 2), (1, 4)), -0.2, 0.2), 0.1, 0.9)
    up_weight = noise(key_of[3], (SECTIONS, PIECES, D, FF_PIECE), D ** -0.5, 0.125, ((0, 2), (1, 4), (3, 2)))
    down_weight = noise(key_of[4], (SECTIONS, PIECES, FF_PIECE, D), FF ** -0.5, 0.0625, ((0, 2), (1, 4), (2, 2)))
    pre_activation = noise(own_keys[5], (SECTIONS, PIECES, PIECES, TOK_DEV, FF_PIECE), 1.0, 6.0, ((0, 2), (1, 4), (4, 2)))
    input_sketch = noise(own_keys[6], (SECTIONS, TOKENS, RANK), 1.0, 6.0, ((0, 2), (1, 4)), jnp.float32)
    model_sketch = noise(key_of[7], (SECTIONS, D, RANK), D ** -0.5, 0.125, ((0, 2),))
    hidden_sketch = noise(key_of[8], (SECTIONS, PIECES, FF_PIECE, RANK), FF ** -0.5, 0.0625, ((0, 2), (1, 4), (2, 2)))
    lengths = jax.vmap(lambda own: ragged_sizes(own, EX_DEV, TOK_DEV, MOST_EX, 2))(jax.random.split(own_keys[9], SECTIONS * PIECES)).reshape((SECTIONS, PIECES, EX_DEV)).astype(jnp.int32)
    return {"cotangent": cotangent, "routes": routes, "gate_values": gate_values, "up_weight": up_weight, "down_weight": down_weight, "pre_activation": pre_activation, "input_sketch": input_sketch, "model_sketch": model_sketch, "hidden_sketch": hidden_sketch, "lengths": lengths}


def expert_rows(rows_in, pre_rows, up_local, down_local, sketch_local):
    pre = pre_rows.astype(jnp.float32)
    sig = jax.nn.sigmoid(pre)
    hidden = (pre * sig).astype(jnp.bfloat16)
    slope = sig * (1.0 + pre * (1.0 - sig))
    grad_hidden = lax.dot_general(rows_in, down_local, (((1,), (1,)), ((), ())), preferred_element_type=jnp.float32)
    grad_pre = (grad_hidden * slope).astype(jnp.bfloat16)
    partial_in = lax.dot_general(grad_pre, up_local, (((1,), (1,)), ((), ())), preferred_element_type=jnp.float32)
    down_part = jnp.dot(hidden, sketch_local, preferred_element_type=jnp.float32)
    up_part = jnp.dot(grad_pre, sketch_local, preferred_element_type=jnp.float32)
    return partial_in, down_part, up_part


def reference(cotangent, routes, gate_values, up_weight, down_weight, pre_activation, input_sketch, model_sketch, hidden_sketch, lengths):
    per_expert = PIECES // EXPERTS
    grads = []
    feats = []
    for section in range(SECTIONS):
        cot = cotangent[section]
        cot_f = cot.astype(jnp.float32)
        token_routes = jnp.repeat(routes[section], BLOCK, axis=0)
        section_gates = gate_values[section]

        def piece_step(carry, piece):
            grad_term, down_vec, up_vec = carry
            expert = piece // per_expert
            weight = jnp.sum(jnp.where(token_routes == expert, section_gates, 0.0), axis=1)
            rows_in = (weight[:, None] * cot_f).astype(jnp.bfloat16)
            pre_rows = lax.dynamic_index_in_dim(pre_activation[section], piece, 0, keepdims=False).reshape(TOKENS, FF_PIECE)
            up_local = lax.dynamic_index_in_dim(up_weight[section], piece, 0, keepdims=False)
            down_local = lax.dynamic_index_in_dim(down_weight[section], piece, 0, keepdims=False)
            sketch_local = lax.dynamic_index_in_dim(hidden_sketch[section], piece, 0, keepdims=False)
            partial_in, down_part, up_part = expert_rows(rows_in, pre_rows, up_local, down_local, sketch_local)
            return (grad_term + partial_in, down_vec + weight[:, None] * down_part, up_vec + up_part), None

        start = (jnp.zeros((TOKENS, D), jnp.float32), jnp.zeros((TOKENS, RANK), jnp.float32), jnp.zeros((TOKENS, RANK), jnp.float32))
        (grad_term, down_vec, up_vec), unused = lax.scan(piece_step, start, jnp.arange(PIECES, dtype=jnp.int32))
        grads.append((cot_f + grad_term).astype(jnp.bfloat16))
        out_vec = jnp.dot(cot, model_sketch[section], preferred_element_type=jnp.float32)
        counts = lengths[section]
        ends = jnp.cumsum(counts, axis=1)
        starts = ends - counts
        position = jnp.arange(TOK_DEV, dtype=jnp.int32)
        member = ((position[None, None, :] >= starts[:, :, None]) & (position[None, None, :] < ends[:, :, None])).astype(jnp.float32)
        down_feat = jnp.einsum("qet,qta,qtb->qeab", member, out_vec.reshape(PIECES, TOK_DEV, RANK), down_vec.reshape(PIECES, TOK_DEV, RANK), precision=lax.Precision.HIGHEST)
        up_feat = jnp.einsum("qet,qta,qtb->qeab", member, up_vec.reshape(PIECES, TOK_DEV, RANK), input_sketch[section].reshape(PIECES, TOK_DEV, RANK), precision=lax.Precision.HIGHEST)
        feats.append(jnp.concatenate([down_feat, up_feat], axis=3).reshape(EXAMPLES, RANK, 2 * RANK))
    handed = jnp.roll(jnp.stack(grads), -1, axis=0)
    return handed, jnp.stack(feats)
```

```python
import functools

import jax
import jax.numpy as jnp
from jax import lax
from jax.experimental import pallas as pl
from jax.experimental.pallas import tpu as pltpu
from jax.sharding import PartitionSpec as P

EXPERTS = 4
F32 = jnp.float32
BF16 = jnp.bfloat16
NT = (((1,), (1,)), ((), ()))


def tile_of(extent, most):
    return max(t for t in range(128, most + 1, 128) if extent % t == 0)


def slots(d, n):
    upper = d // (n // 2)
    edge = d + upper * (n - 1 - 2 * d)
    side = 1 - 2 * upper
    out = [d]
    for i in range(1, n):
        near = (i + 1) // 2 if i % 2 else -(i // 2)
        both = jnp.where(2 * edge >= i, 1, 0)
        out.append(d + side * (both * near + (1 - both) * (i - edge)))
    return out


def kernel(
    n,
    sections,
    group,
    th,
    tn,
    cot_hbm,
    routes_ref,
    gates_ref,
    up_hbm,
    down_hbm,
    pre_hbm,
    insk_ref,
    model_ref,
    sketch_ref,
    len_ref,
    hand_out,
    feat_out,
    cot_all,
    wt_own,
    wt_all,
    slope_v,
    down_v2,
    up_v,
    down_v,
    pre_v,
    rows_v,
    gp_v,
    acc_v,
    mine_v,
    sk_v,
    xsend,
    xrecv,
    ssend,
    srecv,
    osend,
    orecv,
    tsend,
    trecv,
    cot_next,
    sk_sum,
    down_sem,
    up_sem,
    pre_sem,
    own_sem,
    up_send,
    dn_send,
    ag_recv,
    wt_send,
    wt_recv,
    fw_send,
    fw_recv,
    cn_send,
    cn_recv,
    x_send,
    x_recv,
    s_send,
    s_recv,
    o_send,
    o_recv,
    t_send,
    t_recv,
    h_send,
    h_recv,
    k_send,
    k_recv,
):
    tok, width = cot_hbm.shape
    half = tok // 2
    hidden_cols = up_hbm.shape[1]
    rank = insk_ref.shape[0]
    d = lax.axis_index("dp")
    s = lax.axis_index("section")
    c = lax.axis_index("tensor")
    pc = 1 - c
    below = (s + sections - 1) % sections
    above = (s + 1) % sections
    n_groups = n // group
    n_th = hidden_cols // th
    n_tn = width // tn
    blocks = slots(d, n)
    mine_rows = pl.ds(pl.multiple_of(c * half, half), half)
    other_rows = pl.ds(pl.multiple_of(pc * half, half), half)

    def remote(src, dst, ssem, rsem, **to):
        return pltpu.make_async_remote_copy(
            src_ref=src,
            dst_ref=dst,
            send_sem=ssem,
            recv_sem=rsem,
            device_id=to,
            device_id_type=pl.DeviceIdType.MESH,
        )

    own_copy = pltpu.make_async_copy(cot_hbm, cot_all.at[d], own_sem)
    own_copy.start()

    def pre_copy(b, i):
        return pltpu.make_async_copy(pre_hbm.at[b], pre_v.at[b], pre_sem.at[i])

    def down_copy(t):
        rows = pl.ds(pl.multiple_of(t * th, th), th)
        return pltpu.make_async_copy(down_hbm.at[rows], down_v.at[rows], down_sem.at[t])

    def up_copy(t):
        rows = pl.ds(pl.multiple_of(t * tn, tn), tn)
        return pltpu.make_async_copy(up_hbm.at[rows], up_v.at[rows], up_sem.at[t])

    for i in range(n):
        pre_copy(blocks[i], i).start()
    for t in range(n_th):
        down_copy(t).start()
    for t in range(n_tn):
        up_copy(t).start()

    block_rows = routes_ref.shape[0]
    token_block = lax.broadcasted_iota(jnp.int32, (8, tok), 1) // (tok // block_rows)
    for p in range(n):
        expert = p // (n // EXPERTS)
        weight = jnp.zeros((8, tok), F32)
        for q in range(block_rows):
            for k in range(2):
                share = jnp.where(token_block == q, gates_ref[k : k + 1, :], 0.0)
                weight += jnp.where(routes_ref[q, k] == expert, share, 0.0)
        wt_own[p] = weight

    barrier = pltpu.get_barrier_semaphore()
    greet = [{"tensor": pc}]
    greet += [{"dp": blocks[i]} for i in range(1, n)]
    greet += [{"section": below, "dp": blocks[i]} for i in range(n)]
    if sections > 2:
        greet += [{"section": above, "dp": blocks[i]} for i in range(n)]
    for to in greet:
        pl.semaphore_signal(barrier, inc=1, device_id=to, device_id_type=pl.DeviceIdType.MESH)
    pl.semaphore_wait(barrier, len(greet))

    part = half // CHUNKS

    def chunk(core, j):
        return pl.ds(pl.multiple_of(core * half + j * part, part), part)

    def line_copy(b, j, to, send):
        rows = chunk(c, j)
        return remote(
            cot_all.at[b, rows], cot_all.at[b, rows], send.at[b, j], ag_recv.at[b, j], dp=to
        )

    def own_line(j, to, send):
        rows = chunk(c, j)
        return remote(
            cot_hbm.at[rows], cot_all.at[d, rows], send.at[d, j], ag_recv.at[d, j], dp=to
        )

    def up_line(b, j):
        return line_copy(b, j, jnp.minimum(d + 1, n - 1), up_send)

    def down_line(b, j):
        return line_copy(b, j, jnp.maximum(d - 1, 0), dn_send)

    def wt_copy(i, source):
        return remote(
            wt_own.at[blocks[i]], wt_all.at[source], wt_send.at[i], wt_recv.at[source], dp=blocks[i]
        )

    def fw_copy(b, j, core):
        rows = chunk(core, j)
        return remote(
            cot_all.at[b, rows], cot_all.at[b, rows], fw_send.at[b, j], fw_recv.at[b, j], tensor=pc
        )

    cn_copy = remote(cot_hbm.at[mine_rows], cot_next, cn_send, cn_recv, section=below)
    for i in range(1, n):
        wt_copy(i, d).start()

    @pl.when(d < n - 1)
    def _():
        for j in range(CHUNKS):
            own_line(j, d + 1, up_send).start()

    @pl.when(d > 0)
    def _():
        for j in range(CHUNKS):
            own_line(j, d - 1, dn_send).start()

    cn_copy.start()

    def arrive(k, chunks=range(CHUNKS)):
        for j in chunks:

            @pl.when(d >= k)
            def _(j=j):
                up_line(d - k, j).wait_recv()

                @pl.when(d < n - 1)
                def _():
                    up_line(d - k, j).start()

                fw_copy(d - k, j, c).start()

            @pl.when(d + k < n)
            def _(j=j):
                down_line(d + k, j).wait_recv()

                @pl.when(d > 0)
                def _():
                    down_line(d + k, j).start()

                fw_copy(d + k, j, c).start()

    own_copy.wait()
    out_vec_t = lax.dot_general(
        model_ref[...], cot_all[d], NT, preferred_element_type=F32
    )
    wt_all[d] = wt_own[d]
    eye = lax.broadcasted_iota(jnp.int32, (tok, tok), 0) == lax.broadcasted_iota(
        jnp.int32, (tok, tok), 1
    )

    def x_copy(g, t):
        return remote(xsend.at[g, t], xrecv.at[g, t], x_send.at[g, t], x_recv.at[g, t], tensor=pc)

    def s_copy(g):
        return remote(ssend.at[g], srecv.at[g], s_send.at[g], s_recv.at[g], tensor=pc)

    def o_copy(i, t, b, source):
        return remote(
            osend.at[i, t],
            orecv.at[source, t],
            o_send.at[i, t],
            o_recv.at[source, t],
            section=below,
            dp=b,
        )

    def t_copy(i, b, source):
        return remote(tsend.at[i], trecv.at[source], t_send.at[i], t_recv.at[source], dp=b)

    for i in range(n):
        pre_copy(blocks[i], i).wait()
    down_v2[...] = jnp.zeros_like(down_v2)

    def ahead(t, carry):
        rows = pl.ds(pl.multiple_of(t * th, th), th)
        sk = sketch_ref[:, rows]
        for b in range(n):
            pre = pre_v[b, :, rows].astype(F32)
            sig = jax.nn.sigmoid(pre)
            hid = (pre * sig).astype(BF16)
            slope_v[b, :, rows] = sig * (1.0 + pre * (1.0 - sig))
            down_v2[b] += lax.dot_general(hid, sk, NT, preferred_element_type=F32)
        return carry

    lax.fori_loop(0, n_th, ahead, 0)
    arrived = 0
    for g in range(n_groups):
        members = list(range(g * group, (g + 1) * group))
        while arrived < min(members[-1], n - 1):
            arrived += 1
            arrive(arrived)
        for m, i in enumerate(members):
            b = blocks[i]
            if i:
                for j in range(CHUNKS):
                    fw_copy(b, j, pc).wait_recv()
                wt_copy(i, b).wait_recv()
            row = wt_all[b][0:1, :]
            col = jnp.sum(jnp.where(eye, jnp.broadcast_to(row, (tok, tok)), 0.0), axis=1, keepdims=True)
            at = slice(m * tok, (m + 1) * tok)
            rows_v[at, :] = (col * cot_all[b].astype(F32)).astype(BF16)
            sk_v[at, :] = jnp.concatenate([down_v2[b] * col, jnp.zeros((tok, rank), F32)], axis=1)

        def first(t, carry, g=g, members=members):
            if g == 0:
                down_copy(t).wait()
            rows = pl.ds(pl.multiple_of(t * th, th), th)
            gh = lax.dot_general(rows_v[...], down_v[rows, :], NT, preferred_element_type=F32)
            for j, i in enumerate(members):
                at = slice(j * tok, (j + 1) * tok)
                gp_v[at, rows] = (gh[at] * slope_v[blocks[i], :, rows]).astype(BF16)
            return carry

        lax.fori_loop(0, n_th, first, 0)
        if arrived < n - 1:
            arrived += 1
            arrive(arrived)
        sk_v[:, rank:] = lax.dot_general(
            gp_v[...], sketch_ref[...], NT, preferred_element_type=F32
        )
        for j in range(group):
            ssend[g, j * half : (j + 1) * half, :] = sk_v[
                pl.ds(pl.multiple_of(j * tok + pc * half, half), half), :
            ]
        s_copy(g).start()

        far_first = members[::-1] if g == 0 else members

        def pass_on(t, g=g, members=members, far_first=far_first):
            x_copy(g, t).wait_recv()
            cols = pl.ds(pl.multiple_of(t * tn, tn), tn)
            for i in far_first:
                j = members.index(i)
                at = slice(j * half, (j + 1) * half)
                osend[i, t] = (mine_v[at, cols] + xrecv[g, t, at, :].astype(F32)).astype(BF16)
                o_copy(i, t, blocks[i], d).start()

        def sketch_on(g=g, members=members):
            s_copy(g).wait_recv()
            for j, i in enumerate(members):
                at = slice(j * half, (j + 1) * half)
                total = sk_v[pl.ds(pl.multiple_of(j * tok + c * half, half), half), :] + srecv[g, at, :]
                if i:
                    tsend[i] = total
                    t_copy(i, blocks[i], d).start()
                else:
                    sk_sum[mine_rows, :] = total

        def second(t, carry, g=g, pass_on=pass_on, sketch_on=sketch_on):
            if g == 0:
                up_copy(t).wait()
            rows = pl.ds(pl.multiple_of(t * tn, tn), tn)
            acc_v[...] = lax.dot_general(gp_v[...], up_v[rows, :], NT, preferred_element_type=F32)
            for j in range(group):
                at = slice(j * half, (j + 1) * half)
                mine_v[at, rows] = acc_v[pl.ds(pl.multiple_of(j * tok + c * half, half), half), :]
                xsend[g, t, at, :] = acc_v[
                    pl.ds(pl.multiple_of(j * tok + pc * half, half), half), :
                ].astype(BF16)
            x_copy(g, t).start()

            @pl.when(t > 0)
            def _():
                pass_on(t - 1)

            @pl.when(t == 1)
            def _():
                sketch_on()

            return carry

        lax.fori_loop(0, n_tn, second, 0)
        pass_on(n_tn - 1)
    for i in range(1, n):
        t_copy(i, blocks[i], blocks[i]).wait_recv()
        sk_sum[mine_rows, :] += trecv[blocks[i]]

    def k_copy(rows):
        return remote(sk_sum.at[rows], sk_sum.at[rows], k_send, k_recv, tensor=pc)

    k_copy(mine_rows).start()
    k_copy(other_rows).wait_recv()
    sk = sk_sum[...]
    up_vec_t = sk.T[rank:, :]
    position = lax.broadcasted_iota(jnp.int32, (rank, tok), 1)
    left, right = [], []
    begin = jnp.int32(0)
    for e in range(len_ref.shape[0]):
        end = begin + len_ref[e]
        member = (position >= begin) & (position < end)
        left.append(jnp.where(member, out_vec_t, 0.0))
        right.append(jnp.where(member, up_vec_t, 0.0))
        begin = end
    exact = functools.partial(
        jnp.dot, preferred_element_type=F32, precision=lax.Precision.HIGHEST
    )
    down_feat = exact(jnp.concatenate(left, axis=0), sk[:, :rank])
    up_feat = lax.dot_general(
        jnp.concatenate(right, axis=0),
        insk_ref[...],
        NT,
        preferred_element_type=F32,
        precision=lax.Precision.HIGHEST,
    )
    feat_out[...] = jnp.concatenate([down_feat, up_feat], axis=1)

    cn_copy.wait_recv()
    def h_copy(t, rows):
        part = hand_out.at[rows, pl.ds(t * tn, tn)]
        return remote(part, part, h_send.at[t], h_recv.at[t], tensor=pc)

    for t in range(n_tn):
        cols = slice(t * tn, (t + 1) * tn)
        total = cot_next[:, cols].astype(F32)
        for i in range(n):
            o_copy(i, t, blocks[i], blocks[i]).wait_recv()
            total = total + orecv[blocks[i], t].astype(F32)
        hand_out[mine_rows, cols] = total.astype(BF16)
        h_copy(t, mine_rows).start()

    for t in range(n_tn):
        h_copy(t, other_rows).wait_recv()
        h_copy(t, mine_rows).wait_send()
    for i in range(1, n):
        wt_copy(i, d).wait_send()
        t_copy(i, blocks[i], d).wait_send()
    for i in range(n):
        for t in range(n_tn):
            o_copy(i, t, blocks[i], d).wait_send()
    for g in range(n_groups):
        s_copy(g).wait_send()
        for t in range(n_tn):
            x_copy(g, t).wait_send()
    for k in range(n):
        for j in range(CHUNKS):

            @pl.when(d >= k)
            def _(k=k, j=j):
                @pl.when(d < n - 1)
                def _():
                    up_line(d - k, j).wait_send()

                if k:
                    fw_copy(d - k, j, c).wait_send()

            @pl.when(d + k < n)
            def _(k=k, j=j):
                @pl.when(d > 0)
                def _():
                    down_line(d + k, j).wait_send()

                if k:
                    fw_copy(d + k, j, c).wait_send()

    cn_copy.wait_send()
    k_copy(mine_rows).wait_send()


GROUP = 2
CHUNKS = 2


def per_device(
    cotangent,
    routes,
    gate_values,
    up_weight,
    down_weight,
    pre_activation,
    input_sketch,
    model_sketch,
    hidden_sketch,
    lengths,
):
    n = lax.axis_size("dp")
    sections = lax.axis_size("section")
    tok, width = cotangent.shape[1:]
    rank = model_sketch.shape[2]
    hidden_cols = up_weight.shape[3]
    examples = lengths.shape[2]
    group = GROUP
    half = tok // 2
    m = group * tok
    th = tile_of(hidden_cols, 512)
    tn = tile_of(width, 512)
    n_th, n_tn, n_g = hidden_cols // th, width // tn, n // group
    dma = pltpu.SemaphoreType.DMA
    vmem = pl.BlockSpec(memory_space=pltpu.VMEM)
    hbm = pl.BlockSpec(memory_space=pl.ANY)
    hand, feat = pl.pallas_call(
        functools.partial(kernel, n, sections, group, th, tn),
        out_shape=(
            jax.ShapeDtypeStruct((tok, width), BF16),
            jax.ShapeDtypeStruct((examples * rank, 2 * rank), F32),
        ),
        in_specs=[
            hbm,
            pl.BlockSpec(memory_space=pltpu.SMEM),
            vmem,
            hbm,
            hbm,
            hbm,
            vmem,
            vmem,
            vmem,
            pl.BlockSpec(memory_space=pltpu.SMEM),
        ],
        out_specs=(vmem, vmem),
        scratch_shapes=[
            pltpu.VMEM((n, tok, width), BF16),
            pltpu.VMEM((n, 8, tok), F32),
            pltpu.VMEM((n, 8, tok), F32),
            pltpu.VMEM((n, tok, hidden_cols), F32),
            pltpu.VMEM((n, tok, rank), F32),
            pltpu.VMEM((width, hidden_cols), BF16),
            pltpu.VMEM((hidden_cols, width), BF16),
            pltpu.VMEM((n, tok, hidden_cols), BF16),
            pltpu.VMEM((m, width), BF16),
            pltpu.VMEM((m, hidden_cols), BF16),
            pltpu.VMEM((m, tn), F32),
            pltpu.VMEM((m // 2, width), F32),
            pltpu.VMEM((m, 2 * rank), F32),
            pltpu.VMEM((n_g, n_tn, m // 2, tn), BF16),
            pltpu.VMEM((n_g, n_tn, m // 2, tn), BF16),
            pltpu.VMEM((n_g, m // 2, 2 * rank), F32),
            pltpu.VMEM((n_g, m // 2, 2 * rank), F32),
            pltpu.VMEM((n, n_tn, half, tn), BF16),
            pltpu.VMEM((n, n_tn, half, tn), BF16),
            pltpu.VMEM((n, half, 2 * rank), F32),
            pltpu.VMEM((n, half, 2 * rank), F32),
            pltpu.VMEM((half, width), BF16),
            pltpu.VMEM((tok, 2 * rank), F32),
            dma((n_th,)),
            dma((n_tn,)),
            dma((n,)),
            dma(()),
            dma((n, CHUNKS)),
            dma((n, CHUNKS)),
            dma((n, CHUNKS)),
            dma((n,)),
            dma((n,)),
            dma((n, CHUNKS)),
            dma((n, CHUNKS)),
            dma(()),
            dma(()),
            dma((n_g, n_tn)),
            dma((n_g, n_tn)),
            dma((n_g,)),
            dma((n_g,)),
            dma((n, n_tn)),
            dma((n, n_tn)),
            dma((n,)),
            dma((n,)),
            dma((n_tn,)),
            dma((n_tn,)),
            dma(()),
            dma(()),
        ],
        compiler_params=pltpu.CompilerParams(
            collective_id=0, has_side_effects=True, vmem_limit_bytes=63 * 1024 * 1024
        ),
        name="window",
    )(
        cotangent[0],
        routes[0],
        gate_values[0].T,
        up_weight[0, 0],
        down_weight[0, 0],
        pre_activation[0, 0],
        input_sketch[0].T,
        model_sketch[0].T,
        hidden_sketch[0, 0].T,
        lengths[0, 0],
    )
    return (hand[None], feat.reshape(1, examples, rank, 2 * rank))


def solution(mesh):
    in_specs = (
        P("section", ("groups", "dp"), None),
        P("section", ("groups", "dp"), None),
        P("section", ("groups", "dp"), None),
        P("section", "dp", None, "tensor"),
        P("section", "dp", "tensor", None),
        P("section", ("groups", "dp"), None, None, "tensor"),
        P("section", ("groups", "dp"), None),
        P("section", None, None),
        P("section", "dp", "tensor", None),
        P("section", ("groups", "dp"), None),
    )
    out_specs = (P("section", ("groups", "dp"), None), P("section", ("groups", "dp"), None, None))
    return jax.shard_map(
        per_device, mesh=mesh, in_specs=in_specs, out_specs=out_specs, check_vma=False
    )
```

```python
import functools

import jax
import jax.numpy as jnp
from jax import lax
from jax.experimental import pallas as pl
from jax.experimental.pallas import tpu as pltpu
from jax.sharding import PartitionSpec as P

EXPERTS = 4
F32 = jnp.float32
BF16 = jnp.bfloat16
NT = (((1,), (1,)), ((), ()))


def tile_of(extent, most):
    return max(t for t in range(128, most + 1, 128) if extent % t == 0)


def slots(d, n):
    upper = d // (n // 2)
    edge = d + upper * (n - 1 - 2 * d)
    side = 1 - 2 * upper
    out = [d]
    for i in range(1, n):
        near = (i + 1) // 2 if i % 2 else -(i // 2)
        both = jnp.where(2 * edge >= i, 1, 0)
        out.append(d + side * (both * near + (1 - both) * (i - edge)))
    return out


def kernel(
    n,
    sections,
    group,
    th,
    tn,
    cot_hbm,
    routes_ref,
    gates_ref,
    up_hbm,
    down_hbm,
    pre_hbm,
    insk_ref,
    model_ref,
    sketch_ref,
    len_ref,
    hand_out,
    feat_out,
    hand_v,
    feat_v,
    cot_all,
    wt_own,
    wt_all,
    slope_v,
    down_v2,
    up_v,
    down_v,
    pre_v,
    rows_v,
    gp_v,
    acc_v,
    mine_v,
    sk_v,
    xsend,
    xrecv,
    ssend,
    srecv,
    osend,
    orecv,
    tsend,
    trecv,
    cot_next,
    sk_sum,
    comb,
    down_sem,
    up_sem,
    pre_sem,
    own_sem,
    up_send,
    dn_send,
    ag_recv,
    wt_send,
    wt_recv,
    fw_send,
    fw_recv,
    cn_send,
    cn_recv,
    x_send,
    x_recv,
    s_send,
    s_recv,
    o_send,
    o_recv,
    t_send,
    t_recv,
    h_send,
    h_recv,
    k_send,
    k_recv,
    keep_sem,
    feat_sem,
    c_send,
    c_recv,
):
    tok, width = cot_hbm.shape
    half = tok // 2
    hidden_cols = up_hbm.shape[1]
    rank = insk_ref.shape[0]
    d = lax.axis_index("dp")
    s = lax.axis_index("section")
    c = lax.axis_index("tensor")
    pc = 1 - c
    below = (s + sections - 1) % sections
    above = (s + 1) % sections
    n_groups = n // group
    n_th = hidden_cols // th
    n_tn = width // tn
    blocks = slots(d, n)
    mine_rows = pl.ds(pl.multiple_of(c * half, half), half)
    other_rows = pl.ds(pl.multiple_of(pc * half, half), half)

    def remote(src, dst, ssem, rsem, **to):
        return pltpu.make_async_remote_copy(
            src_ref=src,
            dst_ref=dst,
            send_sem=ssem,
            recv_sem=rsem,
            device_id=to,
            device_id_type=pl.DeviceIdType.MESH,
        )

    own_copy = pltpu.make_async_copy(cot_hbm, cot_all.at[d], own_sem)

    def pre_copy(b, i):
        return pltpu.make_async_copy(pre_hbm.at[b], pre_v.at[b], pre_sem.at[i])

    def down_copy(t):
        rows = pl.ds(pl.multiple_of(t * th, th), th)
        return pltpu.make_async_copy(down_hbm.at[rows], down_v.at[rows], down_sem.at[t])

    def up_copy(t):
        rows = pl.ds(pl.multiple_of(t * tn, tn), tn)
        return pltpu.make_async_copy(up_hbm.at[rows], up_v.at[rows], up_sem.at[t])

    for i in range(n):
        pre_copy(blocks[i], i).start()
    own_copy.start()

    block_rows = routes_ref.shape[0]
    token_block = lax.broadcasted_iota(jnp.int32, (8, tok), 1) // (tok // block_rows)
    for p in range(n):
        expert = p // (n // EXPERTS)
        weight = jnp.zeros((8, tok), F32)
        for q in range(block_rows):
            for k in range(2):
                share = jnp.where(token_block == q, gates_ref[k : k + 1, :], 0.0)
                weight += jnp.where(routes_ref[q, k] == expert, share, 0.0)
        wt_own[p] = weight

    barrier = pltpu.get_barrier_semaphore()
    greet = [{"tensor": pc}]
    greet += [{"dp": blocks[i]} for i in range(1, n)]
    greet += [{"section": below, "dp": blocks[i]} for i in range(n)]
    if sections > 2:
        greet += [{"section": above, "dp": blocks[i]} for i in range(n)]
    for to in greet:
        pl.semaphore_signal(barrier, inc=1, device_id=to, device_id_type=pl.DeviceIdType.MESH)
    for i in range(n):
        pre_copy(blocks[i], i).wait()
    for t in range(n_th):
        down_copy(t).start()
    for t in range(n_tn):
        up_copy(t).start()
    pl.semaphore_wait(barrier, len(greet))

    part = half // CHUNKS

    def chunk(core, j):
        return pl.ds(pl.multiple_of(core * half + j * part, part), part)

    def line_copy(b, j, to, send):
        rows = chunk(c, j)
        return remote(
            cot_all.at[b, rows], cot_all.at[b, rows], send.at[b, j], ag_recv.at[b, j], dp=to
        )

    def own_line(j, to, send):
        rows = chunk(c, j)
        return remote(
            cot_all.at[d, rows], cot_all.at[d, rows], send.at[d, j], ag_recv.at[d, j], dp=to
        )

    def up_line(b, j):
        return line_copy(b, j, jnp.minimum(d + 1, n - 1), up_send)

    def down_line(b, j):
        return line_copy(b, j, jnp.maximum(d - 1, 0), dn_send)

    def wt_copy(i, source):
        return remote(
            wt_own.at[blocks[i]], wt_all.at[source], wt_send.at[i], wt_recv.at[source], dp=blocks[i]
        )

    def fw_copy(b, j, core):
        rows = chunk(core, j)
        return remote(
            cot_all.at[b, rows], cot_all.at[b, rows], fw_send.at[b, j], fw_recv.at[b, j], tensor=pc
        )

    cn_copy = remote(cot_all.at[d, mine_rows], cot_next, cn_send, cn_recv, section=below)
    own_copy.wait()
    for i in range(1, n):
        wt_copy(i, d).start()

    @pl.when(d < n - 1)
    def _():
        for j in range(CHUNKS):
            own_line(j, d + 1, up_send).start()

    @pl.when(d > 0)
    def _():
        for j in range(CHUNKS):
            own_line(j, d - 1, dn_send).start()

    cn_copy.start()

    def arrive(k, chunks=range(CHUNKS)):
        for j in chunks:

            @pl.when(d >= k)
            def _(j=j):
                up_line(d - k, j).wait_recv()

                @pl.when(d < n - 1)
                def _():
                    up_line(d - k, j).start()

                fw_copy(d - k, j, c).start()

            @pl.when(d + k < n)
            def _(j=j):
                down_line(d + k, j).wait_recv()

                @pl.when(d > 0)
                def _():
                    down_line(d + k, j).start()

                fw_copy(d + k, j, c).start()

    out_vec_t = lax.dot_general(
        model_ref[...], cot_all[d], NT, preferred_element_type=F32
    )
    wt_all[d] = wt_own[d]
    eye = lax.broadcasted_iota(jnp.int32, (tok, tok), 0) == lax.broadcasted_iota(
        jnp.int32, (tok, tok), 1
    )

    def x_copy(g, t):
        return remote(xsend.at[g, t], xrecv.at[g, t], x_send.at[g, t], x_recv.at[g, t], tensor=pc)

    def s_copy(g):
        return remote(ssend.at[g], srecv.at[g], s_send.at[g], s_recv.at[g], tensor=pc)

    def o_copy(i, t, b, source):
        return remote(
            osend.at[i, t],
            orecv.at[source, t],
            o_send.at[i, t],
            o_recv.at[source, t],
            section=below,
            dp=b,
        )

    last = n - 1
    is_end = (d == 0) | (d == n - 1)
    is_inner = (d != 0) & (d != n - 1) & ((d == 1) | (d == n - 2))
    inner = jnp.where(d == 0, 1, n - 2)

    def c_copy(t):
        return remote(osend.at[last, t], comb.at[t], c_send.at[t], c_recv.at[t], dp=inner)

    def send_out(i, t):
        if i < last:
            o_copy(i, t, blocks[i], d).start()
            return
        pl.when(is_end)(lambda: c_copy(t).start())
        if n > 4:
            pl.when(~is_end & ~is_inner)(lambda: o_copy(i, t, blocks[i], d).start())

    def t_copy(i, b, source):
        return remote(tsend.at[i], trecv.at[source], t_send.at[i], t_recv.at[source], dp=b)

    down_v2[...] = jnp.zeros_like(down_v2)

    def ahead(t, carry):
        rows = pl.ds(pl.multiple_of(t * th, th), th)
        sk = sketch_ref[:, rows]
        for b in range(n):
            pre = pre_v[b, :, rows].astype(F32)
            sig = jax.nn.sigmoid(pre)
            hid = (pre * sig).astype(BF16)
            slope_v[b, :, rows] = sig * (1.0 + pre * (1.0 - sig))
            down_v2[b] += lax.dot_general(hid, sk, NT, preferred_element_type=F32)
        return carry

    lax.fori_loop(0, n_th, ahead, 0)
    arrived = 0
    for g in range(n_groups):
        members = list(range(g * group, (g + 1) * group))
        while arrived < min(members[-1], n - 1):
            arrived += 1
            arrive(arrived)
        for m, i in enumerate(members):
            b = blocks[i]
            if i:
                for j in range(CHUNKS):
                    fw_copy(b, j, pc).wait_recv()
                wt_copy(i, b).wait_recv()
            row = wt_all[b][0:1, :]
            col = jnp.sum(jnp.where(eye, jnp.broadcast_to(row, (tok, tok)), 0.0), axis=1, keepdims=True)
            at = slice(m * tok, (m + 1) * tok)
            rows_v[at, :] = (col * cot_all[b].astype(F32)).astype(BF16)
            sk_v[at, :] = jnp.concatenate([down_v2[b] * col, jnp.zeros((tok, rank), F32)], axis=1)

        def first(t, carry, g=g, members=members):
            if g == 0:
                down_copy(t).wait()
            rows = pl.ds(pl.multiple_of(t * th, th), th)
            gh = lax.dot_general(rows_v[...], down_v[rows, :], NT, preferred_element_type=F32)
            for j, i in enumerate(members):
                at = slice(j * tok, (j + 1) * tok)
                gp_v[at, rows] = (gh[at] * slope_v[blocks[i], :, rows]).astype(BF16)
            return carry

        lax.fori_loop(0, n_th, first, 0)
        if arrived < n - 1:
            arrived += 1
            arrive(arrived)
        far_first = members[::-1]

        def pass_on(t, g=g, members=members, far_first=far_first):
            x_copy(g, t).wait_recv()
            cols = pl.ds(pl.multiple_of(t * tn, tn), tn)
            for i in far_first:
                j = members.index(i)
                at = slice(j * half, (j + 1) * half)
                osend[i, t] = (mine_v[at, cols] + xrecv[g, t, at, :].astype(F32)).astype(BF16)
                send_out(i, t)

        def sketch(g=g):
            sk_v[:, rank:] = lax.dot_general(
                gp_v[...], sketch_ref[...], NT, preferred_element_type=F32
            )
            for j in range(group):
                ssend[g, j * half : (j + 1) * half, :] = sk_v[
                    pl.ds(pl.multiple_of(j * tok + pc * half, half), half), :
                ]
            s_copy(g).start()

        def sketch_on(g=g, members=members):
            s_copy(g).wait_recv()
            for j, i in enumerate(members):
                at = slice(j * half, (j + 1) * half)
                total = sk_v[pl.ds(pl.multiple_of(j * tok + c * half, half), half), :] + srecv[g, at, :]
                if i:
                    tsend[i] = total.astype(BF16)
                    t_copy(i, blocks[i], d).start()
                else:
                    sk_sum[mine_rows, :] = total

        def second(t, carry, g=g, pass_on=pass_on, sketch=sketch, sketch_on=sketch_on):
            if g == 0:
                up_copy(t).wait()
            rows = pl.ds(pl.multiple_of(t * tn, tn), tn)
            acc_v[...] = lax.dot_general(gp_v[...], up_v[rows, :], NT, preferred_element_type=F32)
            for j in range(group):
                at = slice(j * half, (j + 1) * half)
                mine_v[at, rows] = acc_v[pl.ds(pl.multiple_of(j * tok + c * half, half), half), :]
                xsend[g, t, at, :] = acc_v[
                    pl.ds(pl.multiple_of(j * tok + pc * half, half), half), :
                ].astype(BF16)
            x_copy(g, t).start()

            pl.when(t == 0)(sketch)
            pl.when(t == 1)(sketch_on)

            @pl.when(t > 0)
            def _():
                pass_on(t - 1)

            return carry

        lax.fori_loop(0, n_tn, second, 0)
        need = min((g + 2) * group - 1, n - 1)
        while g + 1 < n_groups and arrived < need:
            arrived += 1
            arrive(arrived)
        pass_on(n_tn - 1)

    @pl.when(is_inner)
    def _():
        for t in range(n_tn):
            c_copy(t).wait_recv()
            osend[last, t] = (osend[last, t].astype(F32) + comb[t].astype(F32)).astype(BF16)
            o_copy(last, t, blocks[last], d).start()

    for i in range(1, n):
        t_copy(i, blocks[i], blocks[i]).wait_recv()
        sk_sum[mine_rows, :] += trecv[blocks[i]].astype(F32)

    def k_copy(rows):
        return remote(sk_sum.at[rows], sk_sum.at[rows], k_send, k_recv, tensor=pc)

    k_copy(mine_rows).start()
    k_copy(other_rows).wait_recv()
    sk = sk_sum[...]
    up_vec_t = sk.T[rank:, :]
    position = lax.broadcasted_iota(jnp.int32, (rank, tok), 1)
    left, right = [], []
    begin = jnp.int32(0)
    for e in range(len_ref.shape[0]):
        end = begin + len_ref[e]
        member = (position >= begin) & (position < end)
        left.append(jnp.where(member, out_vec_t, 0.0))
        right.append(jnp.where(member, up_vec_t, 0.0))
        begin = end
    exact = functools.partial(
        jnp.dot, preferred_element_type=F32, precision=lax.Precision.HIGHEST
    )
    down_feat = exact(jnp.concatenate(left, axis=0), sk[:, :rank])
    up_feat = lax.dot_general(
        jnp.concatenate(right, axis=0),
        insk_ref[...],
        NT,
        preferred_element_type=F32,
        precision=lax.Precision.HIGHEST,
    )
    feat_v[...] = jnp.concatenate([down_feat, up_feat], axis=1)
    feat_copy = pltpu.make_async_copy(feat_v, feat_out, feat_sem)
    feat_copy.start()

    cn_copy.wait_recv()
    def h_copy(t, rows):
        cols = pl.ds(t * tn, tn)
        return remote(
            hand_v.at[rows, cols], hand_out.at[rows, cols], h_send.at[t], h_recv.at[t], tensor=pc
        )

    def keep_copy(t):
        cols = pl.ds(t * tn, tn)
        return pltpu.make_async_copy(
            hand_v.at[mine_rows, cols], hand_out.at[mine_rows, cols], keep_sem.at[t]
        )

    for t in range(n_tn):
        cols = slice(t * tn, (t + 1) * tn)
        total = cot_next[:, cols].astype(F32)
        for i in range(last):
            o_copy(i, t, blocks[i], blocks[i]).wait_recv()
            total = total + orecv[blocks[i], t].astype(F32)

        @pl.when(is_end)
        def _(total=total, cols=cols):
            hand_v[mine_rows, cols] = total.astype(BF16)

        @pl.when(~is_end)
        def _(total=total, cols=cols, t=t):
            o_copy(last, t, blocks[last], blocks[last]).wait_recv()
            hand_v[mine_rows, cols] = (total + orecv[blocks[last], t].astype(F32)).astype(BF16)

        h_copy(t, mine_rows).start()
        keep_copy(t).start()

    for t in range(n_tn):
        h_copy(t, other_rows).wait_recv()
        h_copy(t, mine_rows).wait_send()
        keep_copy(t).wait()
    feat_copy.wait()
    for i in range(1, n):
        wt_copy(i, d).wait_send()
        t_copy(i, blocks[i], d).wait_send()
    for t in range(n_tn):
        for i in range(last):
            o_copy(i, t, blocks[i], d).wait_send()
        pl.when(is_end)(lambda t=t: c_copy(t).wait_send())
        pl.when(~is_end)(lambda t=t: o_copy(last, t, blocks[last], d).wait_send())
    for g in range(n_groups):
        s_copy(g).wait_send()
        for t in range(n_tn):
            x_copy(g, t).wait_send()
    for k in range(n):
        for j in range(CHUNKS):

            @pl.when(d >= k)
            def _(k=k, j=j):
                @pl.when(d < n - 1)
                def _():
                    up_line(d - k, j).wait_send()

                if k:
                    fw_copy(d - k, j, c).wait_send()

            @pl.when(d + k < n)
            def _(k=k, j=j):
                @pl.when(d > 0)
                def _():
                    down_line(d + k, j).wait_send()

                if k:
                    fw_copy(d + k, j, c).wait_send()

    cn_copy.wait_send()
    k_copy(mine_rows).wait_send()


GROUP = 2
CHUNKS = 2


def per_device(
    cotangent,
    routes,
    gate_values,
    up_weight,
    down_weight,
    pre_activation,
    input_sketch,
    model_sketch,
    hidden_sketch,
    lengths,
):
    n = lax.axis_size("dp")
    sections = lax.axis_size("section")
    tok, width = cotangent.shape[1:]
    rank = model_sketch.shape[2]
    hidden_cols = up_weight.shape[3]
    examples = lengths.shape[2]
    group = GROUP
    half = tok // 2
    m = group * tok
    th = tile_of(hidden_cols, 512)
    tn = tile_of(width, 512)
    n_th, n_tn, n_g = hidden_cols // th, width // tn, n // group
    dma = pltpu.SemaphoreType.DMA
    vmem = pl.BlockSpec(memory_space=pltpu.VMEM)
    hbm = pl.BlockSpec(memory_space=pl.ANY)
    hand, feat = pl.pallas_call(
        functools.partial(kernel, n, sections, group, th, tn),
        out_shape=(
            jax.ShapeDtypeStruct((tok, width), BF16),
            jax.ShapeDtypeStruct((examples * rank, 2 * rank), F32),
        ),
        in_specs=[
            hbm,
            pl.BlockSpec(memory_space=pltpu.SMEM),
            vmem,
            hbm,
            hbm,
            hbm,
            vmem,
            vmem,
            vmem,
            pl.BlockSpec(memory_space=pltpu.SMEM),
        ],
        out_specs=(hbm, hbm),
        scratch_shapes=[
            pltpu.VMEM((tok, width), BF16),
            pltpu.VMEM((examples * rank, 2 * rank), F32),
            pltpu.VMEM((n, tok, width), BF16),
            pltpu.VMEM((n, 8, tok), F32),
            pltpu.VMEM((n, 8, tok), F32),
            pltpu.VMEM((n, tok, hidden_cols), F32),
            pltpu.VMEM((n, tok, rank), F32),
            pltpu.VMEM((width, hidden_cols), BF16),
            pltpu.VMEM((hidden_cols, width), BF16),
            pltpu.VMEM((n, tok, hidden_cols), BF16),
            pltpu.VMEM((m, width), BF16),
            pltpu.VMEM((m, hidden_cols), BF16),
            pltpu.VMEM((m, tn), F32),
            pltpu.VMEM((m // 2, width), F32),
            pltpu.VMEM((m, 2 * rank), F32),
            pltpu.VMEM((n_g, n_tn, m // 2, tn), BF16),
            pltpu.VMEM((n_g, n_tn, m // 2, tn), BF16),
            pltpu.VMEM((n_g, m // 2, 2 * rank), F32),
            pltpu.VMEM((n_g, m // 2, 2 * rank), F32),
            pltpu.VMEM((n, n_tn, half, tn), BF16),
            pltpu.VMEM((n, n_tn, half, tn), BF16),
            pltpu.VMEM((n, half, 2 * rank), BF16),
            pltpu.VMEM((n, half, 2 * rank), BF16),
            pltpu.VMEM((half, width), BF16),
            pltpu.VMEM((tok, 2 * rank), F32),
            pltpu.VMEM((n_tn, half, tn), BF16),
            dma((n_th,)),
            dma((n_tn,)),
            dma((n,)),
            dma(()),
            dma((n, CHUNKS)),
            dma((n, CHUNKS)),
            dma((n, CHUNKS)),
            dma((n,)),
            dma((n,)),
            dma((n, CHUNKS)),
            dma((n, CHUNKS)),
            dma(()),
            dma(()),
            dma((n_g, n_tn)),
            dma((n_g, n_tn)),
            dma((n_g,)),
            dma((n_g,)),
            dma((n, n_tn)),
            dma((n, n_tn)),
            dma((n,)),
            dma((n,)),
            dma((n_tn,)),
            dma((n_tn,)),
            dma(()),
            dma(()),
            dma((n_tn,)),
            dma(()),
            dma((n_tn,)),
            dma((n_tn,)),
        ],
        compiler_params=pltpu.CompilerParams(
            collective_id=0, has_side_effects=True, vmem_limit_bytes=63 * 1024 * 1024
        ),
        name="window",
    )(
        cotangent[0],
        routes[0],
        gate_values[0].T,
        up_weight[0, 0],
        down_weight[0, 0],
        pre_activation[0, 0],
        input_sketch[0].T,
        model_sketch[0].T,
        hidden_sketch[0, 0].T,
        lengths[0, 0],
    )
    return (hand[None], feat.reshape(1, examples, rank, 2 * rank))


def solution(mesh):
    in_specs = (
        P("section", ("groups", "dp"), None),
        P("section", ("groups", "dp"), None),
        P("section", ("groups", "dp"), None),
        P("section", "dp", None, "tensor"),
        P("section", "dp", "tensor", None),
        P("section", ("groups", "dp"), None, None, "tensor"),
        P("section", ("groups", "dp"), None),
        P("section", None, None),
        P("section", "dp", "tensor", None),
        P("section", ("groups", "dp"), None),
    )
    out_specs = (P("section", ("groups", "dp"), None), P("section", ("groups", "dp"), None, None))
    return jax.shard_map(
        per_device, mesh=mesh, in_specs=in_specs, out_specs=out_specs, check_vma=False
    )
```

```python
import functools

import jax
import jax.numpy as jnp
from jax import lax
from jax.experimental import pallas as pl
from jax.experimental.pallas import tpu as pltpu
from jax.sharding import PartitionSpec as P

EXPERTS = 4
F32 = jnp.float32
BF16 = jnp.bfloat16
NT = (((1,), (1,)), ((), ()))


def tile_of(extent, most):
    return max(t for t in range(128, most + 1, 128) if extent % t == 0)


def slots(d, n):
    upper = d // (n // 2)
    edge = d + upper * (n - 1 - 2 * d)
    side = 1 - 2 * upper
    out = [d]
    for i in range(1, n):
        near = (i + 1) // 2 if i % 2 else -(i // 2)
        both = jnp.where(2 * edge >= i, 1, 0)
        out.append(d + side * (both * near + (1 - both) * (i - edge)))
    return out


def kernel(
    n,
    sections,
    group,
    th,
    tn,
    cot_hbm,
    routes_ref,
    gates_ref,
    up_hbm,
    down_hbm,
    pre_hbm,
    insk_ref,
    model_ref,
    sketch_ref,
    len_ref,
    hand_out,
    feat_out,
    hand_v,
    feat_v,
    cot_all,
    wt_own,
    wt_all,
    slope_v,
    down_v2,
    up_v,
    down_v,
    pre_v,
    rows_v,
    gp_v,
    acc_v,
    mine_v,
    sk_v,
    xsend,
    xrecv,
    ssend,
    srecv,
    osend,
    orecv,
    tsend,
    trecv,
    cot_next,
    sk_sum,
    comb,
    down_sem,
    up_sem,
    pre_sem,
    own_sem,
    up_send,
    dn_send,
    ag_recv,
    wt_send,
    wt_recv,
    fw_send,
    fw_recv,
    cn_send,
    cn_recv,
    x_send,
    x_recv,
    s_send,
    s_recv,
    o_send,
    o_recv,
    t_send,
    t_recv,
    h_send,
    h_recv,
    k_send,
    k_recv,
    keep_sem,
    feat_sem,
    c_send,
    c_recv,
):
    tok, width = cot_hbm.shape
    half = tok // 2
    hidden_cols = up_hbm.shape[1]
    rank = insk_ref.shape[0]
    d = lax.axis_index("dp")
    s = lax.axis_index("section")
    c = lax.axis_index("tensor")
    pc = 1 - c
    below = (s + sections - 1) % sections
    above = (s + 1) % sections
    n_groups = n // group
    n_th = hidden_cols // th
    n_tn = width // tn
    blocks = slots(d, n)
    mine_rows = pl.ds(pl.multiple_of(c * half, half), half)
    other_rows = pl.ds(pl.multiple_of(pc * half, half), half)

    def remote(src, dst, ssem, rsem, **to):
        return pltpu.make_async_remote_copy(
            src_ref=src,
            dst_ref=dst,
            send_sem=ssem,
            recv_sem=rsem,
            device_id=to,
            device_id_type=pl.DeviceIdType.MESH,
        )

    own_copy = pltpu.make_async_copy(cot_hbm, cot_all.at[d], own_sem)

    def pre_copy(b, i):
        return pltpu.make_async_copy(pre_hbm.at[b], pre_v.at[b], pre_sem.at[i])

    def down_copy(t):
        rows = pl.ds(pl.multiple_of(t * th, th), th)
        return pltpu.make_async_copy(down_hbm.at[rows], down_v.at[rows], down_sem.at[t])

    def up_copy(t):
        rows = pl.ds(pl.multiple_of(t * tn, tn), tn)
        return pltpu.make_async_copy(up_hbm.at[rows], up_v.at[rows], up_sem.at[t])

    for i in range(n):
        pre_copy(blocks[i], i).start()
    own_copy.start()

    block_rows = routes_ref.shape[0]
    token_block = lax.broadcasted_iota(jnp.int32, (8, tok), 1) // (tok // block_rows)
    for p in range(n):
        expert = p // (n // EXPERTS)
        weight = jnp.zeros((8, tok), F32)
        for q in range(block_rows):
            for k in range(2):
                share = jnp.where(token_block == q, gates_ref[k : k + 1, :], 0.0)
                weight += jnp.where(routes_ref[q, k] == expert, share, 0.0)
        wt_own[p] = weight

    barrier = pltpu.get_barrier_semaphore()
    greet = [{"tensor": pc}]
    greet += [{"dp": blocks[i]} for i in range(1, n)]
    greet += [{"section": below, "dp": blocks[i]} for i in range(n)]
    if sections > 2:
        greet += [{"section": above, "dp": blocks[i]} for i in range(n)]
    for to in greet:
        pl.semaphore_signal(barrier, inc=1, device_id=to, device_id_type=pl.DeviceIdType.MESH)
    for i in range(n):
        pre_copy(blocks[i], i).wait()
    for t in range(n_th):
        down_copy(t).start()
    for t in range(n_tn):
        up_copy(t).start()
    pl.semaphore_wait(barrier, len(greet))

    part = half // CHUNKS

    def chunk(core, j):
        return pl.ds(pl.multiple_of(core * half + j * part, part), part)

    def line_copy(b, j, to, send):
        rows = chunk(c, j)
        return remote(
            cot_all.at[b, rows], cot_all.at[b, rows], send.at[b, j], ag_recv.at[b, j], dp=to
        )

    def own_line(j, to, send):
        rows = chunk(c, j)
        return remote(
            cot_all.at[d, rows], cot_all.at[d, rows], send.at[d, j], ag_recv.at[d, j], dp=to
        )

    def up_line(b, j):
        return line_copy(b, j, jnp.minimum(d + 1, n - 1), up_send)

    def down_line(b, j):
        return line_copy(b, j, jnp.maximum(d - 1, 0), dn_send)

    def wt_copy(i, source):
        return remote(
            wt_own.at[blocks[i]], wt_all.at[source], wt_send.at[i], wt_recv.at[source], dp=blocks[i]
        )

    def fw_copy(b, j, core):
        rows = chunk(core, j)
        return remote(
            cot_all.at[b, rows], cot_all.at[b, rows], fw_send.at[b, j], fw_recv.at[b, j], tensor=pc
        )

    cn_copy = remote(cot_all.at[d, mine_rows], cot_next, cn_send, cn_recv, section=below)
    own_copy.wait()
    for i in range(1, n):
        wt_copy(i, d).start()

    @pl.when(d < n - 1)
    def _():
        for j in range(CHUNKS):
            own_line(j, d + 1, up_send).start()

    @pl.when(d > 0)
    def _():
        for j in range(CHUNKS):
            own_line(j, d - 1, dn_send).start()

    cn_copy.start()

    is_upper = d >= n // 2

    def arrive(k):
        def take(b, line, may, at_once):
            def pass_chunk(j):
                pl.when(may)(lambda: line(b, j).start())

            def pass_all():
                for j in range(CHUNKS):
                    pass_chunk(j)

            for j in range(CHUNKS):
                line(b, j).wait_recv()
                pl.when(at_once)(lambda j=j: pass_chunk(j))
                fw_copy(b, j, c).start()
            pl.when(~at_once)(pass_all)

        def from_low():
            take(d - k, up_line, d < n - 1, ~is_upper | (k > 1))

        def from_high():
            take(d + k, down_line, d > 0, is_upper | (k > 1))

        pl.when(is_upper & (d >= k))(from_low)
        pl.when(d + k < n)(from_high)
        pl.when(~is_upper & (d >= k))(from_low)

    out_vec_t = lax.dot_general(
        model_ref[...], cot_all[d], NT, preferred_element_type=F32
    )
    wt_all[d] = wt_own[d]
    eye = lax.broadcasted_iota(jnp.int32, (tok, tok), 0) == lax.broadcasted_iota(
        jnp.int32, (tok, tok), 1
    )

    def x_copy(g, t):
        return remote(xsend.at[g, t], xrecv.at[g, t], x_send.at[g, t], x_recv.at[g, t], tensor=pc)

    def s_copy(g):
        return remote(ssend.at[g], srecv.at[g], s_send.at[g], s_recv.at[g], tensor=pc)

    def o_copy(i, t, b, source):
        return remote(
            osend.at[i, t],
            orecv.at[source, t],
            o_send.at[i, t],
            o_recv.at[source, t],
            section=below,
            dp=b,
        )

    last = n - 1
    is_end = (d == 0) | (d == n - 1)
    is_inner = (d != 0) & (d != n - 1) & ((d == 1) | (d == n - 2))
    inner = jnp.where(d == 0, 1, n - 2)

    def c_copy(t):
        return remote(osend.at[last, t], comb.at[t], c_send.at[t], c_recv.at[t], dp=inner)

    def send_out(i, t):
        if i < last:
            o_copy(i, t, blocks[i], d).start()
            return
        pl.when(is_end)(lambda: c_copy(t).start())
        if n > 4:
            pl.when(~is_end & ~is_inner)(lambda: o_copy(i, t, blocks[i], d).start())

    def t_copy(i, b, source):
        return remote(tsend.at[i], trecv.at[source], t_send.at[i], t_recv.at[source], dp=b)

    down_v2[...] = jnp.zeros_like(down_v2)

    def ahead(t, carry):
        rows = pl.ds(pl.multiple_of(t * th, th), th)
        sk = sketch_ref[:, rows]
        for b in range(n):
            pre = pre_v[b, :, rows].astype(F32)
            sig = jax.nn.sigmoid(pre)
            hid = (pre * sig).astype(BF16)
            slope_v[b, :, rows] = sig * (1.0 + pre * (1.0 - sig))
            down_v2[b] += lax.dot_general(hid, sk, NT, preferred_element_type=F32)
        return carry

    lax.fori_loop(0, n_th, ahead, 0)
    arrived = 0
    for g in range(n_groups):
        members = list(range(g * group, (g + 1) * group))
        while arrived < min(members[-1], n - 1):
            arrived += 1
            arrive(arrived)
        for m, i in enumerate(members):
            b = blocks[i]
            if i:
                for j in range(CHUNKS):
                    fw_copy(b, j, pc).wait_recv()
                wt_copy(i, b).wait_recv()
            row = wt_all[b][0:1, :]
            col = jnp.sum(jnp.where(eye, jnp.broadcast_to(row, (tok, tok)), 0.0), axis=1, keepdims=True)
            at = slice(m * tok, (m + 1) * tok)
            rows_v[at, :] = (col * cot_all[b].astype(F32)).astype(BF16)
            sk_v[at, :] = jnp.concatenate([down_v2[b] * col, jnp.zeros((tok, rank), F32)], axis=1)

        def first(t, carry, g=g, members=members):
            if g == 0:
                down_copy(t).wait()
            rows = pl.ds(pl.multiple_of(t * th, th), th)
            gh = lax.dot_general(rows_v[...], down_v[rows, :], NT, preferred_element_type=F32)
            for j, i in enumerate(members):
                at = slice(j * tok, (j + 1) * tok)
                gp_v[at, rows] = (gh[at] * slope_v[blocks[i], :, rows]).astype(BF16)
            return carry

        lax.fori_loop(0, n_th, first, 0)
        if arrived < n - 1:
            arrived += 1
            arrive(arrived)
        far_first = members[::-1]

        def pass_on(t, g=g, members=members, far_first=far_first):
            x_copy(g, t).wait_recv()
            cols = pl.ds(pl.multiple_of(t * tn, tn), tn)
            for i in far_first:
                j = members.index(i)
                at = slice(j * half, (j + 1) * half)
                osend[i, t] = (mine_v[at, cols] + xrecv[g, t, at, :].astype(F32)).astype(BF16)
                send_out(i, t)

        def sketch(g=g):
            sk_v[:, rank:] = lax.dot_general(
                gp_v[...], sketch_ref[...], NT, preferred_element_type=F32
            )
            for j in range(group):
                ssend[g, j * half : (j + 1) * half, :] = sk_v[
                    pl.ds(pl.multiple_of(j * tok + pc * half, half), half), :
                ]
            s_copy(g).start()

        def sketch_on(g=g, members=members):
            s_copy(g).wait_recv()
            for j, i in enumerate(members):
                at = slice(j * half, (j + 1) * half)
                total = sk_v[pl.ds(pl.multiple_of(j * tok + c * half, half), half), :] + srecv[g, at, :]
                if i:
                    tsend[i] = total.astype(BF16)
                    t_copy(i, blocks[i], d).start()
                else:
                    sk_sum[mine_rows, :] = total

        def second(t, carry, g=g, pass_on=pass_on, sketch=sketch, sketch_on=sketch_on):
            if g == 0:
                up_copy(t).wait()
            rows = pl.ds(pl.multiple_of(t * tn, tn), tn)
            acc_v[...] = lax.dot_general(gp_v[...], up_v[rows, :], NT, preferred_element_type=F32)
            for j in range(group):
                at = slice(j * half, (j + 1) * half)
                mine_v[at, rows] = acc_v[pl.ds(pl.multiple_of(j * tok + c * half, half), half), :]
                xsend[g, t, at, :] = acc_v[
                    pl.ds(pl.multiple_of(j * tok + pc * half, half), half), :
                ].astype(BF16)
            x_copy(g, t).start()

            @pl.when(t == 0)
            def _():
                sketch()
                pass_on(0)

            pl.when(t == 1)(sketch_on)

            @pl.when(t > 1)
            def _():
                pass_on(t - 1)

            return carry

        lax.fori_loop(0, n_tn, second, 0)
        need = min((g + 2) * group - 1, n - 1)
        while g + 1 < n_groups and arrived < need:
            arrived += 1
            arrive(arrived)
        if n_tn > 1:
            pass_on(n_tn - 1)

    @pl.when(is_inner)
    def _():
        for t in range(n_tn):
            c_copy(t).wait_recv()
            osend[last, t] = (osend[last, t].astype(F32) + comb[t].astype(F32)).astype(BF16)
            o_copy(last, t, blocks[last], d).start()

    for i in range(1, n):
        t_copy(i, blocks[i], blocks[i]).wait_recv()
        sk_sum[mine_rows, :] += trecv[blocks[i]].astype(F32)

    def k_copy(rows):
        return remote(sk_sum.at[rows], sk_sum.at[rows], k_send, k_recv, tensor=pc)

    k_copy(mine_rows).start()
    k_copy(other_rows).wait_recv()
    sk = sk_sum[...]
    up_vec_t = sk.T[rank:, :]
    position = lax.broadcasted_iota(jnp.int32, (rank, tok), 1)
    left, right = [], []
    begin = jnp.int32(0)
    for e in range(len_ref.shape[0]):
        end = begin + len_ref[e]
        member = (position >= begin) & (position < end)
        left.append(jnp.where(member, out_vec_t, 0.0))
        right.append(jnp.where(member, up_vec_t, 0.0))
        begin = end
    exact = functools.partial(
        jnp.dot, preferred_element_type=F32, precision=lax.Precision.HIGHEST
    )
    down_feat = exact(jnp.concatenate(left, axis=0), sk[:, :rank])
    up_feat = lax.dot_general(
        jnp.concatenate(right, axis=0),
        insk_ref[...],
        NT,
        preferred_element_type=F32,
        precision=lax.Precision.HIGHEST,
    )
    feat_v[...] = jnp.concatenate([down_feat, up_feat], axis=1)
    feat_copy = pltpu.make_async_copy(feat_v, feat_out, feat_sem)
    feat_copy.start()

    cn_copy.wait_recv()
    def h_copy(t, rows):
        cols = pl.ds(t * tn, tn)
        return remote(
            hand_v.at[rows, cols], hand_out.at[rows, cols], h_send.at[t], h_recv.at[t], tensor=pc
        )

    def keep_copy(t):
        cols = pl.ds(t * tn, tn)
        return pltpu.make_async_copy(
            hand_v.at[mine_rows, cols], hand_out.at[mine_rows, cols], keep_sem.at[t]
        )

    for t in range(n_tn):
        cols = slice(t * tn, (t + 1) * tn)
        total = cot_next[:, cols].astype(F32)
        for i in range(last):
            o_copy(i, t, blocks[i], blocks[i]).wait_recv()
            total = total + orecv[blocks[i], t].astype(F32)

        @pl.when(is_end)
        def _(total=total, cols=cols):
            hand_v[mine_rows, cols] = total.astype(BF16)

        @pl.when(~is_end)
        def _(total=total, cols=cols, t=t):
            o_copy(last, t, blocks[last], blocks[last]).wait_recv()
            hand_v[mine_rows, cols] = (total + orecv[blocks[last], t].astype(F32)).astype(BF16)

        h_copy(t, mine_rows).start()
        keep_copy(t).start()

    for t in range(n_tn):
        h_copy(t, other_rows).wait_recv()
        h_copy(t, mine_rows).wait_send()
        keep_copy(t).wait()
    feat_copy.wait()
    for i in range(1, n):
        wt_copy(i, d).wait_send()
        t_copy(i, blocks[i], d).wait_send()
    for t in range(n_tn):
        for i in range(last):
            o_copy(i, t, blocks[i], d).wait_send()
        pl.when(is_end)(lambda t=t: c_copy(t).wait_send())
        pl.when(~is_end)(lambda t=t: o_copy(last, t, blocks[last], d).wait_send())
    for g in range(n_groups):
        s_copy(g).wait_send()
        for t in range(n_tn):
            x_copy(g, t).wait_send()
    for k in range(n):
        for j in range(CHUNKS):

            @pl.when(d >= k)
            def _(k=k, j=j):
                @pl.when(d < n - 1)
                def _():
                    up_line(d - k, j).wait_send()

                if k:
                    fw_copy(d - k, j, c).wait_send()

            @pl.when(d + k < n)
            def _(k=k, j=j):
                @pl.when(d > 0)
                def _():
                    down_line(d + k, j).wait_send()

                if k:
                    fw_copy(d + k, j, c).wait_send()

    cn_copy.wait_send()
    k_copy(mine_rows).wait_send()


def hand_over(parts, hand_in, feat_in, hand_out, feat_out, hand_v, feat_v, in_sem, out_sem):
    rows = hand_in.shape[0] // parts
    into = [pltpu.make_async_copy(feat_in, feat_v, in_sem.at[parts])]
    out = [pltpu.make_async_copy(feat_v, feat_out, out_sem.at[parts])]
    for j in range(parts):
        at = pl.ds(j * rows, rows)
        into.append(pltpu.make_async_copy(hand_in.at[at], hand_v.at[at], in_sem.at[j]))
        out.append(pltpu.make_async_copy(hand_v.at[at], hand_out.at[at], out_sem.at[j]))
    for copy in into:
        copy.start()
    for copy, then in zip(into, out):
        copy.wait()
        then.start()
    for copy in out:
        copy.wait()


GROUP = 2
PARTS = 2
CHUNKS = 2


def per_device(
    cotangent,
    routes,
    gate_values,
    up_weight,
    down_weight,
    pre_activation,
    input_sketch,
    model_sketch,
    hidden_sketch,
    lengths,
):
    n = lax.axis_size("dp")
    sections = lax.axis_size("section")
    tok, width = cotangent.shape[1:]
    rank = model_sketch.shape[2]
    hidden_cols = up_weight.shape[3]
    examples = lengths.shape[2]
    group = GROUP
    half = tok // 2
    m = group * tok
    th = tile_of(hidden_cols, 512)
    tn = tile_of(width, 512)
    n_th, n_tn, n_g = hidden_cols // th, width // tn, n // group
    dma = pltpu.SemaphoreType.DMA
    vmem = pl.BlockSpec(memory_space=pltpu.VMEM)
    hbm = pl.BlockSpec(memory_space=pl.ANY)
    hand, feat = pl.pallas_call(
        functools.partial(kernel, n, sections, group, th, tn),
        out_shape=(
            jax.ShapeDtypeStruct((tok, width), BF16),
            jax.ShapeDtypeStruct((examples * rank, 2 * rank), F32),
        ),
        in_specs=[
            hbm,
            pl.BlockSpec(memory_space=pltpu.SMEM),
            vmem,
            hbm,
            hbm,
            hbm,
            vmem,
            vmem,
            vmem,
            pl.BlockSpec(memory_space=pltpu.SMEM),
        ],
        out_specs=(hbm, hbm),
        scratch_shapes=[
            pltpu.VMEM((tok, width), BF16),
            pltpu.VMEM((examples * rank, 2 * rank), F32),
            pltpu.VMEM((n, tok, width), BF16),
            pltpu.VMEM((n, 8, tok), F32),
            pltpu.VMEM((n, 8, tok), F32),
            pltpu.VMEM((n, tok, hidden_cols), F32),
            pltpu.VMEM((n, tok, rank), F32),
            pltpu.VMEM((width, hidden_cols), BF16),
            pltpu.VMEM((hidden_cols, width), BF16),
            pltpu.VMEM((n, tok, hidden_cols), BF16),
            pltpu.VMEM((m, width), BF16),
            pltpu.VMEM((m, hidden_cols), BF16),
            pltpu.VMEM((m, tn), F32),
            pltpu.VMEM((m // 2, width), F32),
            pltpu.VMEM((m, 2 * rank), F32),
            pltpu.VMEM((n_g, n_tn, m // 2, tn), BF16),
            pltpu.VMEM((n_g, n_tn, m // 2, tn), BF16),
            pltpu.VMEM((n_g, m // 2, 2 * rank), F32),
            pltpu.VMEM((n_g, m // 2, 2 * rank), F32),
            pltpu.VMEM((n, n_tn, half, tn), BF16),
            pltpu.VMEM((n, n_tn, half, tn), BF16),
            pltpu.VMEM((n, half, 2 * rank), BF16),
            pltpu.VMEM((n, half, 2 * rank), BF16),
            pltpu.VMEM((half, width), BF16),
            pltpu.VMEM((tok, 2 * rank), F32),
            pltpu.VMEM((n_tn, half, tn), BF16),
            dma((n_th,)),
            dma((n_tn,)),
            dma((n,)),
            dma(()),
            dma((n, CHUNKS)),
            dma((n, CHUNKS)),
            dma((n, CHUNKS)),
            dma((n,)),
            dma((n,)),
            dma((n, CHUNKS)),
            dma((n, CHUNKS)),
            dma(()),
            dma(()),
            dma((n_g, n_tn)),
            dma((n_g, n_tn)),
            dma((n_g,)),
            dma((n_g,)),
            dma((n, n_tn)),
            dma((n, n_tn)),
            dma((n,)),
            dma((n,)),
            dma((n_tn,)),
            dma((n_tn,)),
            dma(()),
            dma(()),
            dma((n_tn,)),
            dma(()),
            dma((n_tn,)),
            dma((n_tn,)),
        ],
        compiler_params=pltpu.CompilerParams(
            collective_id=0, has_side_effects=True, vmem_limit_bytes=63 * 1024 * 1024
        ),
        name="window",
    )(
        cotangent[0],
        routes[0],
        gate_values[0].T,
        up_weight[0, 0],
        down_weight[0, 0],
        pre_activation[0, 0],
        input_sketch[0].T,
        model_sketch[0].T,
        hidden_sketch[0, 0].T,
        lengths[0, 0],
    )
    hand, feat = pl.pallas_call(
        functools.partial(hand_over, PARTS),
        out_shape=(
            jax.ShapeDtypeStruct(hand.shape, BF16),
            jax.ShapeDtypeStruct(feat.shape, F32),
        ),
        in_specs=[hbm, hbm],
        out_specs=(hbm, hbm),
        scratch_shapes=[
            pltpu.VMEM(hand.shape, BF16),
            pltpu.VMEM(feat.shape, F32),
            dma((PARTS + 1,)),
            dma((PARTS + 1,)),
        ],
        name="hand_over",
    )(hand, feat)
    return (hand[None], feat.reshape(1, examples, rank, 2 * rank))


def solution(mesh):
    in_specs = (
        P("section", ("groups", "dp"), None),
        P("section", ("groups", "dp"), None),
        P("section", ("groups", "dp"), None),
        P("section", "dp", None, "tensor"),
        P("section", "dp", "tensor", None),
        P("section", ("groups", "dp"), None, None, "tensor"),
        P("section", ("groups", "dp"), None),
        P("section", None, None),
        P("section", "dp", "tensor", None),
        P("section", ("groups", "dp"), None),
    )
    out_specs = (P("section", ("groups", "dp"), None), P("section", ("groups", "dp"), None, None))
    return jax.shard_map(
        per_device, mesh=mesh, in_specs=in_specs, out_specs=out_specs, check_vma=False
    )
```

```python
import functools

import jax
import jax.numpy as jnp
from jax import lax
from jax.experimental import pallas as pl
from jax.experimental.pallas import tpu as pltpu
from jax.sharding import PartitionSpec as P

EXPERTS = 4
F32 = jnp.float32
BF16 = jnp.bfloat16
NT = (((1,), (1,)), ((), ()))


def tile_of(extent, most):
    return max(t for t in range(128, most + 1, 128) if extent % t == 0)


def slots(d, n):
    upper = d // (n // 2)
    edge = d + upper * (n - 1 - 2 * d)
    side = 1 - 2 * upper
    out = [d]
    for i in range(1, n):
        near = (i + 1) // 2 if i % 2 else -(i // 2)
        both = jnp.where(2 * edge >= i, 1, 0)
        out.append(d + side * (both * near + (1 - both) * (i - edge)))
    return out


def kernel(
    n,
    sections,
    group,
    th,
    tn,
    cot_hbm,
    routes_ref,
    gates_ref,
    up_hbm,
    down_hbm,
    pre_hbm,
    insk_ref,
    model_ref,
    sketch_ref,
    len_ref,
    hand_out,
    feat_out,
    hand_v,
    feat_v,
    cot_all,
    wt_own,
    wt_all,
    slope_v,
    down_v2,
    up_v,
    down_v,
    pre_v,
    rows_v,
    gp_v,
    acc_v,
    mine_v,
    sk_v,
    xsend,
    xrecv,
    ssend,
    srecv,
    osend,
    orecv,
    tsend,
    trecv,
    cot_next,
    sk_sum,
    comb,
    down_sem,
    up_sem,
    pre_sem,
    own_sem,
    up_send,
    dn_send,
    ag_recv,
    wt_send,
    wt_recv,
    fw_send,
    fw_recv,
    cn_send,
    cn_recv,
    x_send,
    x_recv,
    s_send,
    s_recv,
    o_send,
    o_recv,
    t_send,
    t_recv,
    h_send,
    h_recv,
    k_send,
    k_recv,
    keep_sem,
    feat_sem,
    c_recv,
):
    tok, width = cot_hbm.shape
    half = tok // 2
    hidden_cols = up_hbm.shape[1]
    rank = insk_ref.shape[0]
    d = lax.axis_index("dp")
    s = lax.axis_index("section")
    c = lax.axis_index("tensor")
    pc = 1 - c
    below = (s + sections - 1) % sections
    above = (s + 1) % sections
    n_groups = n // group
    n_th = hidden_cols // th
    n_tn = width // tn
    blocks = slots(d, n)
    mine_rows = pl.ds(pl.multiple_of(c * half, half), half)
    other_rows = pl.ds(pl.multiple_of(pc * half, half), half)

    def remote(src, dst, ssem, rsem, **to):
        return pltpu.make_async_remote_copy(
            src_ref=src,
            dst_ref=dst,
            send_sem=ssem,
            recv_sem=rsem,
            device_id=to,
            device_id_type=pl.DeviceIdType.MESH,
        )

    own_copy = pltpu.make_async_copy(cot_hbm, cot_all.at[d], own_sem)

    def pre_copy(b, i):
        return pltpu.make_async_copy(pre_hbm.at[b], pre_v.at[b], pre_sem)

    def down_copy(t):
        rows = pl.ds(pl.multiple_of(t * th, th), th)
        return pltpu.make_async_copy(down_hbm.at[rows], down_v.at[rows], down_sem.at[t])

    def up_copy(t):
        rows = pl.ds(pl.multiple_of(t * tn, tn), tn)
        return pltpu.make_async_copy(up_hbm.at[rows], up_v.at[rows], up_sem.at[t])

    for i in range(n):
        pre_copy(blocks[i], i).start()
    own_copy.start()

    block_rows = routes_ref.shape[0]
    token_block = lax.broadcasted_iota(jnp.int32, (8, tok), 1) // (tok // block_rows)
    for p in range(n):
        expert = p // (n // EXPERTS)
        weight = jnp.zeros((8, tok), F32)
        for q in range(block_rows):
            for k in range(2):
                share = jnp.where(token_block == q, gates_ref[k : k + 1, :], 0.0)
                weight += jnp.where(routes_ref[q, k] == expert, share, 0.0)
        wt_own[p] = weight

    barrier = pltpu.get_barrier_semaphore()
    greet = [{"tensor": pc}]
    greet += [{"dp": blocks[i]} for i in range(1, n)]
    greet += [{"section": below, "dp": blocks[i]} for i in range(n)]
    if sections > 2:
        greet += [{"section": above, "dp": blocks[i]} for i in range(n)]
    for to in greet:
        pl.semaphore_signal(barrier, inc=1, device_id=to, device_id_type=pl.DeviceIdType.MESH)
    pl.semaphore_wait(barrier, len(greet))

    part = half // CHUNKS

    def chunk(core, j):
        return pl.ds(pl.multiple_of(core * half + j * part, part), part)

    def line_copy(b, j, to, send):
        rows = chunk(c, j)
        return remote(
            cot_all.at[b, rows], cot_all.at[b, rows], send, ag_recv.at[b, j], dp=to
        )

    def own_line(j, to, send):
        rows = chunk(c, j)
        return remote(
            cot_hbm.at[rows], cot_all.at[d, rows], send, ag_recv.at[d, j], dp=to
        )

    def up_line(b, j):
        return line_copy(b, j, jnp.minimum(d + 1, n - 1), up_send)

    def down_line(b, j):
        return line_copy(b, j, jnp.maximum(d - 1, 0), dn_send)

    def wt_copy(i, source):
        return remote(
            wt_own.at[blocks[i]], wt_all.at[source], wt_send, wt_recv.at[source], dp=blocks[i]
        )

    def fw_copy(b, j, core):
        rows = chunk(core, j)
        return remote(
            cot_all.at[b, rows], cot_all.at[b, rows], fw_send, fw_recv.at[b, j], tensor=pc
        )

    cn_copy = remote(cot_hbm.at[mine_rows], cot_next, cn_send, cn_recv, section=below)
    for i in range(1, n):
        wt_copy(i, d).start()

    @pl.when(d < n - 1)
    def _():
        for j in range(CHUNKS):
            own_line(j, d + 1, up_send).start()

    @pl.when(d > 0)
    def _():
        for j in range(CHUNKS):
            own_line(j, d - 1, dn_send).start()

    cn_copy.start()
    pltpu.make_async_copy(pre_hbm, pre_v, pre_sem).wait()
    for t in range(n_th):
        down_copy(t).start()
    for t in range(n_tn):
        up_copy(t).start()
    own_copy.wait()

    is_upper = d >= n // 2

    def arrive(k):
        def take(b, line, may, at_once):
            def pass_chunk(j):
                pl.when(may)(lambda: line(b, j).start())

            def pass_all():
                for j in range(CHUNKS):
                    pass_chunk(j)

            for j in range(CHUNKS):
                line(b, j).wait_recv()
                pl.when(at_once)(lambda j=j: pass_chunk(j))
                fw_copy(b, j, c).start()
            pl.when(~at_once)(pass_all)

        def from_low():
            take(d - k, up_line, d < n - 1, ~is_upper | (k > 1))

        def from_high():
            take(d + k, down_line, d > 0, is_upper | (k > 1))

        pl.when(is_upper & (d >= k))(from_low)
        pl.when(d + k < n)(from_high)
        pl.when(~is_upper & (d >= k))(from_low)

    out_vec_t = lax.dot_general(
        model_ref[...], cot_all[d], NT, preferred_element_type=F32
    )
    wt_all[d] = wt_own[d]
    eye = lax.broadcasted_iota(jnp.int32, (tok, tok), 0) == lax.broadcasted_iota(
        jnp.int32, (tok, tok), 1
    )

    def x_copy(g, t):
        return remote(xsend.at[g, t], xrecv.at[g, t], x_send, x_recv.at[g, t], tensor=pc)

    def s_copy(g):
        return remote(ssend.at[g], srecv.at[g], s_send, s_recv.at[g], tensor=pc)

    def o_copy(i, t, b, source):
        return remote(
            osend.at[i, t],
            orecv.at[t, source],
            o_send,
            o_recv.at[t],
            section=below,
            dp=b,
        )

    last = n - 1
    is_end = (d == 0) | (d == n - 1)
    is_inner = (d != 0) & (d != n - 1) & ((d == 1) | (d == n - 2))
    inner = jnp.where(d == 0, 1, n - 2)

    piece = half // SPLIT

    def c_copy(t, k):
        rows = pl.ds(k * piece, piece)
        return remote(
            osend.at[last, t, rows], comb.at[t, rows], o_send, c_recv.at[t, k], dp=inner
        )

    def c_start(t):
        for k in range(SPLIT):
            c_copy(t, k).start()

    def c_onward(t, k):
        rows = pl.ds(k * piece, piece)
        b = blocks[last]
        return remote(
            osend.at[last, t, rows],
            orecv.at[t, d, rows],
            o_send,
            o_recv.at[t],
            section=below,
            dp=b,
        )

    def send_out(i, t):
        if i < last:
            o_copy(i, t, blocks[i], d).start()
            return
        pl.when(is_end)(lambda: c_start(t))
        if n > 4:
            pl.when(~is_end & ~is_inner)(lambda: o_copy(i, t, blocks[i], d).start())

    def t_copy(i, b, source):
        return remote(tsend.at[i], trecv.at[source], t_send, t_recv, dp=b)

    down_v2[...] = jnp.zeros_like(down_v2)

    def ahead(t, carry):
        rows = pl.ds(pl.multiple_of(t * th, th), th)
        sk = sketch_ref[:, rows]
        for b in range(n):
            pre = pre_v[b, :, rows].astype(F32)
            sig = jax.nn.sigmoid(pre)
            hid = (pre * sig).astype(BF16)
            slope_v[b, :, rows] = sig * (1.0 + pre * (1.0 - sig))
            down_v2[b] += lax.dot_general(hid, sk, NT, preferred_element_type=F32)
        return carry

    lax.fori_loop(0, n_th, ahead, 0)
    arrived = 0
    for g in range(n_groups):
        members = list(range(g * group, (g + 1) * group))
        while arrived < min(members[-1], n - 1):
            arrived += 1
            arrive(arrived)
        for m, i in enumerate(members):
            b = blocks[i]
            if i:
                for j in range(CHUNKS):
                    fw_copy(b, j, pc).wait_recv()
                wt_copy(i, b).wait_recv()
            row = wt_all[b][0:1, :]
            col = jnp.sum(jnp.where(eye, jnp.broadcast_to(row, (tok, tok)), 0.0), axis=1, keepdims=True)
            at = slice(m * tok, (m + 1) * tok)
            rows_v[at, :] = (col * cot_all[b].astype(F32)).astype(BF16)
            sk_v[at, :] = jnp.concatenate([down_v2[b] * col, jnp.zeros((tok, rank), F32)], axis=1)

        def first(t, carry, g=g, members=members):
            if g == 0:
                down_copy(t).wait()
            rows = pl.ds(pl.multiple_of(t * th, th), th)
            gh = lax.dot_general(rows_v[...], down_v[rows, :], NT, preferred_element_type=F32)
            for j, i in enumerate(members):
                at = slice(j * tok, (j + 1) * tok)
                gp_v[at, rows] = (gh[at] * slope_v[blocks[i], :, rows]).astype(BF16)
            return carry

        lax.fori_loop(0, n_th, first, 0)
        if arrived < n - 1:
            arrived += 1
            arrive(arrived)
        far_first = members[::-1]

        def pass_on(t, g=g, members=members, far_first=far_first):
            x_copy(g, t).wait_recv()
            cols = pl.ds(pl.multiple_of(t * tn, tn), tn)
            for i in far_first:
                j = members.index(i)
                at = slice(j * half, (j + 1) * half)
                osend[i, t] = (mine_v[at, cols] + xrecv[g, t, at, :].astype(F32)).astype(BF16)
                send_out(i, t)

        def sketch(g=g):
            sk_v[:, rank:] = lax.dot_general(
                gp_v[...], sketch_ref[...], NT, preferred_element_type=F32
            )
            for j in range(group):
                ssend[g, j * half : (j + 1) * half, :] = sk_v[
                    pl.ds(pl.multiple_of(j * tok + pc * half, half), half), :
                ]
            s_copy(g).start()

        def sketch_on(g=g, members=members):
            s_copy(g).wait_recv()
            for j, i in enumerate(members):
                at = slice(j * half, (j + 1) * half)
                total = sk_v[pl.ds(pl.multiple_of(j * tok + c * half, half), half), :] + srecv[g, at, :]
                if i:
                    tsend[i] = total.astype(BF16)
                    t_copy(i, blocks[i], d).start()
                else:
                    sk_sum[mine_rows, :] = total

        def second(t, carry, g=g, pass_on=pass_on, sketch=sketch, sketch_on=sketch_on):
            if g == 0:
                up_copy(t).wait()
            rows = pl.ds(pl.multiple_of(t * tn, tn), tn)
            acc_v[...] = lax.dot_general(gp_v[...], up_v[rows, :], NT, preferred_element_type=F32)
            for j in range(group):
                at = slice(j * half, (j + 1) * half)
                mine_v[at, rows] = acc_v[pl.ds(pl.multiple_of(j * tok + c * half, half), half), :]
                xsend[g, t, at, :] = acc_v[
                    pl.ds(pl.multiple_of(j * tok + pc * half, half), half), :
                ].astype(BF16)
            x_copy(g, t).start()

            @pl.when(t == 0)
            def _():
                sketch()
                pass_on(0)

            pl.when(t == 1)(sketch_on)

            @pl.when(t > 1)
            def _():
                pass_on(t - 1)

            return carry

        lax.fori_loop(0, n_tn, second, 0)
        need = min((g + 2) * group - 1, n - 1)
        while g + 1 < n_groups and arrived < need:
            arrived += 1
            arrive(arrived)
        if n_tn > 1:
            pass_on(n_tn - 1)

    @pl.when(is_inner)
    def _():
        for t in range(n_tn):
            for k in range(SPLIT):
                rows = slice(k * piece, (k + 1) * piece)
                c_copy(t, k).wait_recv()
                osend[last, t, rows] = (
                    osend[last, t, rows].astype(F32) + comb[t, rows].astype(F32)
                ).astype(BF16)
                c_onward(t, k).start()

    parts = pl.ds(0, n - 1)
    remote(tsend.at[parts], trecv.at[parts], t_send, t_recv, dp=blocks[1]).wait_recv()
    for i in range(1, n):
        sk_sum[mine_rows, :] += trecv[blocks[i]].astype(F32)

    def k_copy(rows):
        return remote(sk_sum.at[rows], sk_sum.at[rows], k_send, k_recv, tensor=pc)

    k_copy(mine_rows).start()
    k_copy(other_rows).wait_recv()
    sk = sk_sum[...]
    up_vec_t = sk.T[rank:, :]
    position = lax.broadcasted_iota(jnp.int32, (rank, tok), 1)
    left, right = [], []
    begin = jnp.int32(0)
    for e in range(len_ref.shape[0]):
        end = begin + len_ref[e]
        member = (position >= begin) & (position < end)
        left.append(jnp.where(member, out_vec_t, 0.0))
        right.append(jnp.where(member, up_vec_t, 0.0))
        begin = end
    exact = functools.partial(
        jnp.dot, preferred_element_type=F32, precision=lax.Precision.HIGHEST
    )
    down_feat = exact(jnp.concatenate(left, axis=0), sk[:, :rank])
    up_feat = lax.dot_general(
        jnp.concatenate(right, axis=0),
        insk_ref[...],
        NT,
        preferred_element_type=F32,
        precision=lax.Precision.HIGHEST,
    )
    feat_v[...] = jnp.concatenate([down_feat, up_feat], axis=1)
    feat_copy = pltpu.make_async_copy(feat_v, feat_out, feat_sem)
    feat_copy.start()

    cn_copy.wait_recv()
    def h_copy(t, rows):
        cols = pl.ds(t * tn, tn)
        return remote(
            hand_v.at[rows, cols], hand_out.at[rows, cols], h_send, h_recv, tensor=pc
        )

    def keep_copy(t):
        cols = pl.ds(t * tn, tn)
        return pltpu.make_async_copy(
            hand_v.at[mine_rows, cols], hand_out.at[mine_rows, cols], keep_sem
        )

    for t in range(n_tn):
        cols = slice(t * tn, (t + 1) * tn)

        def landed(count, t=t):
            box = orecv.at[t, pl.ds(0, count)]
            remote(box, box, o_send, o_recv.at[t], section=below).wait_recv()

        pl.when(is_end)(functools.partial(landed, n - 1))
        pl.when(~is_end)(functools.partial(landed, n))
        total = cot_next[:, cols].astype(F32)
        for i in range(last):
            total = total + orecv[t, blocks[i]].astype(F32)

        @pl.when(is_end)
        def _(total=total, cols=cols):
            hand_v[mine_rows, cols] = total.astype(BF16)

        @pl.when(~is_end)
        def _(total=total, cols=cols, t=t):
            hand_v[mine_rows, cols] = (total + orecv[t, blocks[last]].astype(F32)).astype(BF16)

        h_copy(t, mine_rows).start()
        keep_copy(t).start()

    remote(hand_v.at[other_rows], hand_out.at[other_rows], h_send, h_recv, tensor=pc).wait_recv()
    remote(hand_v.at[mine_rows], hand_out.at[mine_rows], h_send, h_recv, tensor=pc).wait_send()
    pltpu.make_async_copy(hand_v.at[mine_rows], hand_out.at[mine_rows], keep_sem).wait()
    feat_copy.wait()

    def drain(ref, sem):
        remote(ref, ref, sem, sem, tensor=pc).wait_send()

    drain(wt_own.at[parts], wt_send)
    drain(tsend.at[parts], t_send)
    drain(osend, o_send)
    drain(ssend, s_send)
    drain(xsend, x_send)
    drain(cot_all.at[parts, pl.ds(0, half)], fw_send)
    for m in range(1, n):
        rows = cot_all.at[pl.ds(0, m), pl.ds(0, half)]
        pl.when(d == m - 1)(functools.partial(drain, rows, up_send))
        pl.when(d == n - m)(functools.partial(drain, rows, dn_send))
    cn_copy.wait_send()
    k_copy(mine_rows).wait_send()


def hand_over(parts, hand_in, feat_in, hand_out, feat_out, hand_v, feat_v, in_sem, out_sem):
    rows = hand_in.shape[0] // parts
    into = [pltpu.make_async_copy(feat_in, feat_v, in_sem.at[parts])]
    out = [pltpu.make_async_copy(feat_v, feat_out, out_sem.at[parts])]
    for j in range(parts):
        at = pl.ds(j * rows, rows)
        into.append(pltpu.make_async_copy(hand_in.at[at], hand_v.at[at], in_sem.at[j]))
        out.append(pltpu.make_async_copy(hand_v.at[at], hand_out.at[at], out_sem.at[j]))
    for copy in into:
        copy.start()
    for copy, then in zip(into, out):
        copy.wait()
        then.start()
    for copy in out:
        copy.wait()


GROUP = 2
SPLIT = 1
PARTS = 1
CHUNKS = 2


def per_device(
    cotangent,
    routes,
    gate_values,
    up_weight,
    down_weight,
    pre_activation,
    input_sketch,
    model_sketch,
    hidden_sketch,
    lengths,
):
    n = lax.axis_size("dp")
    sections = lax.axis_size("section")
    tok, width = cotangent.shape[1:]
    rank = model_sketch.shape[2]
    hidden_cols = up_weight.shape[3]
    examples = lengths.shape[2]
    group = GROUP
    half = tok // 2
    m = group * tok
    th = tile_of(hidden_cols, 512)
    tn = tile_of(width, 512)
    n_th, n_tn, n_g = hidden_cols // th, width // tn, n // group
    dma = pltpu.SemaphoreType.DMA
    vmem = pl.BlockSpec(memory_space=pltpu.VMEM)
    hbm = pl.BlockSpec(memory_space=pl.ANY)
    hand, feat = pl.pallas_call(
        functools.partial(kernel, n, sections, group, th, tn),
        out_shape=(
            jax.ShapeDtypeStruct((tok, width), BF16),
            jax.ShapeDtypeStruct((examples * rank, 2 * rank), F32),
        ),
        in_specs=[
            hbm,
            pl.BlockSpec(memory_space=pltpu.SMEM),
            vmem,
            hbm,
            hbm,
            hbm,
            vmem,
            vmem,
            vmem,
            pl.BlockSpec(memory_space=pltpu.SMEM),
        ],
        out_specs=(hbm, hbm),
        scratch_shapes=[
            pltpu.VMEM((tok, width), BF16),
            pltpu.VMEM((examples * rank, 2 * rank), F32),
            pltpu.VMEM((n, tok, width), BF16),
            pltpu.VMEM((n, 8, tok), F32),
            pltpu.VMEM((n, 8, tok), F32),
            pltpu.VMEM((n, tok, hidden_cols), F32),
            pltpu.VMEM((n, tok, rank), F32),
            pltpu.VMEM((width, hidden_cols), BF16),
            pltpu.VMEM((hidden_cols, width), BF16),
            pltpu.VMEM((n, tok, hidden_cols), BF16),
            pltpu.VMEM((m, width), BF16),
            pltpu.VMEM((m, hidden_cols), BF16),
            pltpu.VMEM((m, tn), F32),
            pltpu.VMEM((m // 2, width), F32),
            pltpu.VMEM((m, 2 * rank), F32),
            pltpu.VMEM((n_g, n_tn, m // 2, tn), BF16),
            pltpu.VMEM((n_g, n_tn, m // 2, tn), BF16),
            pltpu.VMEM((n_g, m // 2, 2 * rank), F32),
            pltpu.VMEM((n_g, m // 2, 2 * rank), F32),
            pltpu.VMEM((n, n_tn, half, tn), BF16),
            pltpu.VMEM((n_tn, n, half, tn), BF16),
            pltpu.VMEM((n, half, 2 * rank), BF16),
            pltpu.VMEM((n, half, 2 * rank), BF16),
            pltpu.VMEM((half, width), BF16),
            pltpu.VMEM((tok, 2 * rank), F32),
            pltpu.VMEM((n_tn, half, tn), BF16),
            dma((n_th,)),
            dma((n_tn,)),
            dma(()),
            dma(()),
            dma(()),
            dma(()),
            dma((n, CHUNKS)),
            dma(()),
            dma((n,)),
            dma(()),
            dma((n, CHUNKS)),
            dma(()),
            dma(()),
            dma(()),
            dma((n_g, n_tn)),
            dma(()),
            dma((n_g,)),
            dma(()),
            dma((n_tn,)),
            dma(()),
            dma(()),
            dma(()),
            dma(()),
            dma(()),
            dma(()),
            dma(()),
            dma(()),
            dma((n_tn, SPLIT)),
        ],
        compiler_params=pltpu.CompilerParams(
            collective_id=0, has_side_effects=True, vmem_limit_bytes=63 * 1024 * 1024
        ),
        name="window",
    )(
        cotangent[0],
        routes[0],
        gate_values[0].T,
        up_weight[0, 0],
        down_weight[0, 0],
        pre_activation[0, 0],
        input_sketch[0].T,
        model_sketch[0].T,
        hidden_sketch[0, 0].T,
        lengths[0, 0],
    )
    hand, feat = pl.pallas_call(
        functools.partial(hand_over, PARTS),
        out_shape=(
            jax.ShapeDtypeStruct(hand.shape, BF16),
            jax.ShapeDtypeStruct(feat.shape, F32),
        ),
        in_specs=[hbm, hbm],
        out_specs=(hbm, hbm),
        scratch_shapes=[
            pltpu.VMEM(hand.shape, BF16),
            pltpu.VMEM(feat.shape, F32),
            dma((PARTS + 1,)),
            dma((PARTS + 1,)),
        ],
        name="hand_over",
    )(hand, feat)
    return (hand[None], feat.reshape(1, examples, rank, 2 * rank))


def solution(mesh):
    in_specs = (
        P("section", ("groups", "dp"), None),
        P("section", ("groups", "dp"), None),
        P("section", ("groups", "dp"), None),
        P("section", "dp", None, "tensor"),
        P("section", "dp", "tensor", None),
        P("section", ("groups", "dp"), None, None, "tensor"),
        P("section", ("groups", "dp"), None),
        P("section", None, None),
        P("section", "dp", "tensor", None),
        P("section", ("groups", "dp"), None),
    )
    out_specs = (P("section", ("groups", "dp"), None), P("section", ("groups", "dp"), None, None))
    return jax.shard_map(
        per_device, mesh=mesh, in_specs=in_specs, out_specs=out_specs, check_vma=False
    )
```

```python
import functools

import jax
import jax.numpy as jnp
from jax import lax
from jax.experimental import pallas as pl
from jax.experimental.pallas import tpu as pltpu
from jax.sharding import PartitionSpec as P

EXPERTS = 4
F32 = jnp.float32
BF16 = jnp.bfloat16
NT = (((1,), (1,)), ((), ()))


def tile_of(extent, most):
    return max(t for t in range(128, most + 1, 128) if extent % t == 0)


def slots(d, n):
    upper = d // (n // 2)
    edge = d + upper * (n - 1 - 2 * d)
    side = 1 - 2 * upper
    out = [d]
    for i in range(1, n):
        near = (i + 1) // 2 if i % 2 else -(i // 2)
        both = jnp.where(2 * edge >= i, 1, 0)
        out.append(d + side * (both * near + (1 - both) * (i - edge)))
    return out


def kernel(
    n,
    sections,
    group,
    th,
    tn,
    cot_hbm,
    routes_hbm,
    gates_hbm,
    up_hbm,
    down_hbm,
    pre_hbm,
    insk_hbm,
    model_hbm,
    sketch_hbm,
    len_hbm,
    hand_out,
    feat_out,
    hand_v,
    feat_v,
    cot_all,
    wt_own,
    wt_all,
    slope_v,
    down_v2,
    up_v,
    down_v,
    pre_v,
    rows_v,
    gp_v,
    acc_v,
    mine_v,
    sk_v,
    xsend,
    xrecv,
    ssend,
    srecv,
    osend,
    orecv,
    tsend,
    trecv,
    cot_next,
    sk_sum,
    comb,
    down_sem,
    up_sem,
    pre_sem,
    own_sem,
    up_send,
    dn_send,
    ag_recv,
    wt_send,
    wt_recv,
    fw_send,
    fw_recv,
    cn_send,
    cn_recv,
    x_send,
    x_recv,
    s_send,
    s_recv,
    o_send,
    o_recv,
    t_send,
    t_recv,
    h_send,
    h_recv,
    k_send,
    k_recv,
    keep_sem,
    feat_sem,
    c_recv,
    routes_ref,
    gates_ref,
    insk_ref,
    model_ref,
    sketch_ref,
    len_ref,
    small_sem,
):
    tok, width = cot_hbm.shape
    half = tok // 2
    hidden_cols = up_hbm.shape[1]
    rank = insk_hbm.shape[0]
    d = lax.axis_index("dp")
    s = lax.axis_index("section")
    c = lax.axis_index("tensor")
    pc = 1 - c
    below = (s + sections - 1) % sections
    above = (s + 1) % sections
    n_groups = n // group
    n_th = hidden_cols // th
    n_tn = width // tn
    blocks = slots(d, n)
    mine_rows = pl.ds(pl.multiple_of(c * half, half), half)
    other_rows = pl.ds(pl.multiple_of(pc * half, half), half)

    def remote(src, dst, ssem, rsem, **to):
        return pltpu.make_async_remote_copy(
            src_ref=src,
            dst_ref=dst,
            send_sem=ssem,
            recv_sem=rsem,
            device_id=to,
            device_id_type=pl.DeviceIdType.MESH,
        )

    barrier = pltpu.get_barrier_semaphore()
    greet = [{"tensor": pc}]
    greet += [{"dp": blocks[i]} for i in range(1, n)]
    greet += [{"section": below, "dp": blocks[i]} for i in range(n)]
    if sections > 2:
        greet += [{"section": above, "dp": blocks[i]} for i in range(n)]
    for to in greet:
        pl.semaphore_signal(barrier, inc=1, device_id=to, device_id_type=pl.DeviceIdType.MESH)
    small = [
        pltpu.make_async_copy(source, kept, small_sem.at[i])
        for i, (source, kept) in enumerate(
            (
                (routes_hbm, routes_ref),
                (gates_hbm, gates_ref),
                (sketch_hbm, sketch_ref),
                (model_hbm, model_ref),
                (insk_hbm, insk_ref),
                (len_hbm, len_ref),
            )
        )
    ]
    own_copy = pltpu.make_async_copy(cot_hbm, cot_all.at[d], own_sem)

    def pre_copy(b, i):
        return pltpu.make_async_copy(pre_hbm.at[b], pre_v.at[b], pre_sem)

    def down_copy(t):
        rows = pl.ds(pl.multiple_of(t * th, th), th)
        return pltpu.make_async_copy(down_hbm.at[rows], down_v.at[rows], down_sem.at[t])

    def up_copy(t):
        rows = pl.ds(pl.multiple_of(t * tn, tn), tn)
        return pltpu.make_async_copy(up_hbm.at[rows], up_v.at[rows], up_sem.at[t])

    for i in range(n):
        pre_copy(blocks[i], i).start()
    own_copy.start()
    for copy in small:
        copy.start()

    pl.semaphore_wait(barrier, len(greet))

    part = half // CHUNKS

    def chunk(core, j):
        return pl.ds(pl.multiple_of(core * half + j * part, part), part)

    def line_copy(b, j, to, send):
        rows = chunk(c, j)
        return remote(
            cot_all.at[b, rows], cot_all.at[b, rows], send, ag_recv.at[b, j], dp=to
        )

    def own_line(j, to, send):
        rows = chunk(c, j)
        return remote(
            cot_hbm.at[rows], cot_all.at[d, rows], send, ag_recv.at[d, j], dp=to
        )

    def up_line(b, j):
        return line_copy(b, j, jnp.minimum(d + 1, n - 1), up_send)

    def down_line(b, j):
        return line_copy(b, j, jnp.maximum(d - 1, 0), dn_send)

    def wt_copy(i, source):
        return remote(
            wt_own.at[blocks[i]], wt_all.at[source], wt_send, wt_recv.at[source], dp=blocks[i]
        )

    def fw_copy(b, j, core):
        rows = chunk(core, j)
        return remote(
            cot_all.at[b, rows], cot_all.at[b, rows], fw_send, fw_recv.at[b, j], tensor=pc
        )

    cn_copy = remote(cot_hbm.at[mine_rows], cot_next, cn_send, cn_recv, section=below)

    @pl.when(d < n - 1)
    def _():
        for j in range(CHUNKS):
            own_line(j, d + 1, up_send).start()

    @pl.when(d > 0)
    def _():
        for j in range(CHUNKS):
            own_line(j, d - 1, dn_send).start()

    cn_copy.start()
    pltpu.make_async_copy(pre_hbm, pre_v, pre_sem).wait()
    for t in range(n_th):
        down_copy(t).start()
    for t in range(n_tn):
        up_copy(t).start()
    for copy in small:
        copy.wait()
    block_rows = routes_ref.shape[0]
    token_block = lax.broadcasted_iota(jnp.int32, (8, tok), 1) // (tok // block_rows)
    for p in range(n):
        expert = p // (n // EXPERTS)
        weight = jnp.zeros((8, tok), F32)
        for q in range(block_rows):
            for k in range(2):
                share = jnp.where(token_block == q, gates_ref[k : k + 1, :], 0.0)
                weight += jnp.where(routes_ref[q, k] == expert, share, 0.0)
        wt_own[p] = weight

    for i in range(1, n):
        wt_copy(i, d).start()
    own_copy.wait()

    is_upper = d >= n // 2

    def arrive(k):
        def take(b, line, may, at_once):
            def pass_chunk(j):
                pl.when(may)(lambda: line(b, j).start())

            def pass_all():
                for j in range(CHUNKS):
                    pass_chunk(j)

            for j in range(CHUNKS):
                line(b, j).wait_recv()
                pl.when(at_once)(lambda j=j: pass_chunk(j))
                fw_copy(b, j, c).start()
            pl.when(~at_once)(pass_all)

        def from_low():
            take(d - k, up_line, d < n - 1, ~is_upper | (k > 1))

        def from_high():
            take(d + k, down_line, d > 0, is_upper | (k > 1))

        pl.when(is_upper & (d >= k))(from_low)
        pl.when(d + k < n)(from_high)
        pl.when(~is_upper & (d >= k))(from_low)

    out_vec_t = lax.dot_general(
        model_ref[...], cot_all[d], NT, preferred_element_type=F32
    )
    wt_all[d] = wt_own[d]
    eye = lax.broadcasted_iota(jnp.int32, (tok, tok), 0) == lax.broadcasted_iota(
        jnp.int32, (tok, tok), 1
    )

    def x_copy(g, t):
        return remote(xsend.at[g, t], xrecv.at[g, t], x_send, x_recv.at[g, t], tensor=pc)

    def s_copy(g):
        return remote(ssend.at[g], srecv.at[g], s_send, s_recv.at[g], tensor=pc)

    def o_copy(i, t, b, source):
        return remote(
            osend.at[i, t],
            orecv.at[t, source],
            o_send,
            o_recv.at[t],
            section=below,
            dp=b,
        )

    last = n - 1
    is_end = (d == 0) | (d == n - 1)
    is_inner = (d != 0) & (d != n - 1) & ((d == 1) | (d == n - 2))
    inner = jnp.where(d == 0, 1, n - 2)

    piece = half // SPLIT

    def c_copy(t, k):
        rows = pl.ds(k * piece, piece)
        return remote(
            osend.at[last, t, rows], comb.at[t, rows], o_send, c_recv.at[t, k], dp=inner
        )

    def c_start(t):
        for k in range(SPLIT):
            c_copy(t, k).start()

    def c_onward(t, k):
        rows = pl.ds(k * piece, piece)
        b = blocks[last]
        return remote(
            osend.at[last, t, rows],
            orecv.at[t, d, rows],
            o_send,
            o_recv.at[t],
            section=below,
            dp=b,
        )

    def send_out(i, t):
        if i < last:
            o_copy(i, t, blocks[i], d).start()
            return
        pl.when(is_end)(lambda: c_start(t))
        if n > 4:
            pl.when(~is_end & ~is_inner)(lambda: o_copy(i, t, blocks[i], d).start())

    def t_copy(i, b, source):
        return remote(tsend.at[i], trecv.at[source], t_send, t_recv, dp=b)

    down_v2[...] = jnp.zeros_like(down_v2)

    def ahead(t, carry):
        rows = pl.ds(pl.multiple_of(t * th, th), th)
        sk = sketch_ref[:, rows]
        for b in range(n):
            pre = pre_v[b, :, rows].astype(F32)
            sig = jax.nn.sigmoid(pre)
            hid = (pre * sig).astype(BF16)
            slope_v[b, :, rows] = sig * (1.0 + pre * (1.0 - sig))
            down_v2[b] += lax.dot_general(hid, sk, NT, preferred_element_type=F32)
        return carry

    lax.fori_loop(0, n_th, ahead, 0)
    arrived = 0
    for g in range(n_groups):
        members = list(range(g * group, (g + 1) * group))
        while arrived < min(members[-1], n - 1):
            arrived += 1
            arrive(arrived)
        for m, i in enumerate(members):
            b = blocks[i]
            if i:
                for j in range(CHUNKS):
                    fw_copy(b, j, pc).wait_recv()
                wt_copy(i, b).wait_recv()
            row = wt_all[b][0:1, :]
            col = jnp.sum(jnp.where(eye, jnp.broadcast_to(row, (tok, tok)), 0.0), axis=1, keepdims=True)
            at = slice(m * tok, (m + 1) * tok)
            rows_v[at, :] = (col * cot_all[b].astype(F32)).astype(BF16)
            sk_v[at, :] = jnp.concatenate([down_v2[b] * col, jnp.zeros((tok, rank), F32)], axis=1)

        def first(t, carry, g=g, members=members):
            if g == 0:
                down_copy(t).wait()
            rows = pl.ds(pl.multiple_of(t * th, th), th)
            gh = lax.dot_general(rows_v[...], down_v[rows, :], NT, preferred_element_type=F32)
            for j, i in enumerate(members):
                at = slice(j * tok, (j + 1) * tok)
                gp_v[at, rows] = (gh[at] * slope_v[blocks[i], :, rows]).astype(BF16)
            return carry

        lax.fori_loop(0, n_th, first, 0)
        if arrived < n - 1:
            arrived += 1
            arrive(arrived)
        far_first = members[::-1]

        def pass_on(t, g=g, members=members, far_first=far_first):
            x_copy(g, t).wait_recv()
            cols = pl.ds(pl.multiple_of(t * tn, tn), tn)
            for i in far_first:
                j = members.index(i)
                at = slice(j * half, (j + 1) * half)
                osend[i, t] = (mine_v[at, cols] + xrecv[g, t, at, :].astype(F32)).astype(BF16)
                send_out(i, t)

        def sketch(g=g):
            sk_v[:, rank:] = lax.dot_general(
                gp_v[...], sketch_ref[...], NT, preferred_element_type=F32
            )
            for j in range(group):
                ssend[g, j * half : (j + 1) * half, :] = sk_v[
                    pl.ds(pl.multiple_of(j * tok + pc * half, half), half), :
                ]
            s_copy(g).start()

        def sketch_on(g=g, members=members):
            s_copy(g).wait_recv()
            for j, i in enumerate(members):
                at = slice(j * half, (j + 1) * half)
                total = sk_v[pl.ds(pl.multiple_of(j * tok + c * half, half), half), :] + srecv[g, at, :]
                if i:
                    tsend[i] = total.astype(BF16)
                    t_copy(i, blocks[i], d).start()
                else:
                    sk_sum[mine_rows, :] = total

        def second(t, carry, g=g, pass_on=pass_on, sketch=sketch, sketch_on=sketch_on):
            if g == 0:
                up_copy(t).wait()
            rows = pl.ds(pl.multiple_of(t * tn, tn), tn)
            acc_v[...] = lax.dot_general(gp_v[...], up_v[rows, :], NT, preferred_element_type=F32)
            for j in range(group):
                at = slice(j * half, (j + 1) * half)
                mine_v[at, rows] = acc_v[pl.ds(pl.multiple_of(j * tok + c * half, half), half), :]
                xsend[g, t, at, :] = acc_v[
                    pl.ds(pl.multiple_of(j * tok + pc * half, half), half), :
                ].astype(BF16)
            x_copy(g, t).start()

            @pl.when(t == 0)
            def _():
                sketch()
                pass_on(0)

            pl.when(t == 1)(sketch_on)

            @pl.when(t > 1)
            def _():
                pass_on(t - 1)

            return carry

        lax.fori_loop(0, n_tn, second, 0)
        need = min((g + 2) * group - 1, n - 1)
        while g + 1 < n_groups and arrived < need:
            arrived += 1
            arrive(arrived)
        if n_tn > 1:
            pass_on(n_tn - 1)

    @pl.when(is_inner)
    def _():
        for t in range(n_tn):
            for k in range(SPLIT):
                rows = slice(k * piece, (k + 1) * piece)
                c_copy(t, k).wait_recv()
                osend[last, t, rows] = (
                    osend[last, t, rows].astype(F32) + comb[t, rows].astype(F32)
                ).astype(BF16)
                c_onward(t, k).start()

    parts = pl.ds(0, n - 1)
    remote(tsend.at[parts], trecv.at[parts], t_send, t_recv, dp=blocks[1]).wait_recv()
    for i in range(1, n):
        sk_sum[mine_rows, :] += trecv[blocks[i]].astype(F32)

    def k_copy(rows):
        return remote(sk_sum.at[rows], sk_sum.at[rows], k_send, k_recv, tensor=pc)

    k_copy(mine_rows).start()
    k_copy(other_rows).wait_recv()
    sk = sk_sum[...]
    up_vec_t = sk.T[rank:, :]
    position = lax.broadcasted_iota(jnp.int32, (rank, tok), 1)
    left, right = [], []
    begin = jnp.int32(0)
    for e in range(len_ref.shape[0]):
        end = begin + len_ref[e]
        member = (position >= begin) & (position < end)
        left.append(jnp.where(member, out_vec_t, 0.0))
        right.append(jnp.where(member, up_vec_t, 0.0))
        begin = end
    exact = functools.partial(
        jnp.dot, preferred_element_type=F32, precision=lax.Precision.HIGHEST
    )
    down_feat = exact(jnp.concatenate(left, axis=0), sk[:, :rank])
    up_feat = lax.dot_general(
        jnp.concatenate(right, axis=0),
        insk_ref[...],
        NT,
        preferred_element_type=F32,
        precision=lax.Precision.HIGHEST,
    )
    feat_v[...] = jnp.concatenate([down_feat, up_feat], axis=1)
    feat_copy = pltpu.make_async_copy(feat_v, feat_out, feat_sem)
    feat_copy.start()

    cn_copy.wait_recv()
    def h_copy(t, rows):
        cols = pl.ds(t * tn, tn)
        return remote(
            hand_v.at[rows, cols], hand_out.at[rows, cols], h_send, h_recv, tensor=pc
        )

    def keep_copy(t):
        cols = pl.ds(t * tn, tn)
        return pltpu.make_async_copy(
            hand_v.at[mine_rows, cols], hand_out.at[mine_rows, cols], keep_sem
        )

    for t in range(n_tn):
        cols = slice(t * tn, (t + 1) * tn)

        def landed(count, t=t):
            box = orecv.at[t, pl.ds(0, count)]
            remote(box, box, o_send, o_recv.at[t], section=below).wait_recv()

        pl.when(is_end)(functools.partial(landed, n - 1))
        pl.when(~is_end)(functools.partial(landed, n))
        total = cot_next[:, cols].astype(F32)
        for i in range(last):
            total = total + orecv[t, blocks[i]].astype(F32)

        @pl.when(is_end)
        def _(total=total, cols=cols):
            hand_v[mine_rows, cols] = total.astype(BF16)

        @pl.when(~is_end)
        def _(total=total, cols=cols, t=t):
            hand_v[mine_rows, cols] = (total + orecv[t, blocks[last]].astype(F32)).astype(BF16)

        h_copy(t, mine_rows).start()
        keep_copy(t).start()

    remote(hand_v.at[other_rows], hand_out.at[other_rows], h_send, h_recv, tensor=pc).wait_recv()
    remote(hand_v.at[mine_rows], hand_out.at[mine_rows], h_send, h_recv, tensor=pc).wait_send()
    pltpu.make_async_copy(hand_v.at[mine_rows], hand_out.at[mine_rows], keep_sem).wait()
    feat_copy.wait()

    def drain(ref, sem):
        remote(ref, ref, sem, sem, tensor=pc).wait_send()

    drain(wt_own.at[parts], wt_send)
    drain(tsend.at[parts], t_send)
    drain(osend, o_send)
    drain(ssend, s_send)
    drain(xsend, x_send)
    drain(cot_all.at[parts, pl.ds(0, half)], fw_send)
    for m in range(1, n):
        rows = cot_all.at[pl.ds(0, m), pl.ds(0, half)]
        pl.when(d == m - 1)(functools.partial(drain, rows, up_send))
        pl.when(d == n - m)(functools.partial(drain, rows, dn_send))
    cn_copy.wait_send()
    k_copy(mine_rows).wait_send()


def hand_over(parts, hand_in, feat_in, hand_out, feat_out, hand_v, feat_v, in_sem, out_sem):
    rows = hand_in.shape[0] // parts
    into = [pltpu.make_async_copy(feat_in, feat_v, in_sem.at[parts])]
    out = [pltpu.make_async_copy(feat_v, feat_out, out_sem.at[parts])]
    for j in range(parts):
        at = pl.ds(j * rows, rows)
        into.append(pltpu.make_async_copy(hand_in.at[at], hand_v.at[at], in_sem.at[j]))
        out.append(pltpu.make_async_copy(hand_v.at[at], hand_out.at[at], out_sem.at[j]))
    for copy in into:
        copy.start()
    for copy, then in zip(into, out):
        copy.wait()
        then.start()
    for copy in out:
        copy.wait()


GROUP = 2
SPLIT = 1
PARTS = 1
CHUNKS = 2


def per_device(
    cotangent,
    routes,
    gate_values,
    up_weight,
    down_weight,
    pre_activation,
    input_sketch,
    model_sketch,
    hidden_sketch,
    lengths,
):
    n = lax.axis_size("dp")
    sections = lax.axis_size("section")
    tok, width = cotangent.shape[1:]
    rank = model_sketch.shape[2]
    hidden_cols = up_weight.shape[3]
    examples = lengths.shape[2]
    group = GROUP
    half = tok // 2
    m = group * tok
    th = tile_of(hidden_cols, 512)
    tn = tile_of(width, 512)
    n_th, n_tn, n_g = hidden_cols // th, width // tn, n // group
    dma = pltpu.SemaphoreType.DMA
    hbm = pl.BlockSpec(memory_space=pl.ANY)
    hand, feat = pl.pallas_call(
        functools.partial(kernel, n, sections, group, th, tn),
        out_shape=(
            jax.ShapeDtypeStruct((tok, width), BF16),
            jax.ShapeDtypeStruct((examples * rank, 2 * rank), F32),
        ),
        in_specs=[hbm] * 10,
        out_specs=(hbm, hbm),
        scratch_shapes=[
            pltpu.VMEM((tok, width), BF16),
            pltpu.VMEM((examples * rank, 2 * rank), F32),
            pltpu.VMEM((n, tok, width), BF16),
            pltpu.VMEM((n, 8, tok), F32),
            pltpu.VMEM((n, 8, tok), F32),
            pltpu.VMEM((n, tok, hidden_cols), F32),
            pltpu.VMEM((n, tok, rank), F32),
            pltpu.VMEM((width, hidden_cols), BF16),
            pltpu.VMEM((hidden_cols, width), BF16),
            pltpu.VMEM((n, tok, hidden_cols), BF16),
            pltpu.VMEM((m, width), BF16),
            pltpu.VMEM((m, hidden_cols), BF16),
            pltpu.VMEM((m, tn), F32),
            pltpu.VMEM((m // 2, width), F32),
            pltpu.VMEM((m, 2 * rank), F32),
            pltpu.VMEM((n_g, n_tn, m // 2, tn), BF16),
            pltpu.VMEM((n_g, n_tn, m // 2, tn), BF16),
            pltpu.VMEM((n_g, m // 2, 2 * rank), F32),
            pltpu.VMEM((n_g, m // 2, 2 * rank), F32),
            pltpu.VMEM((n, n_tn, half, tn), BF16),
            pltpu.VMEM((n_tn, n, half, tn), BF16),
            pltpu.VMEM((n, half, 2 * rank), BF16),
            pltpu.VMEM((n, half, 2 * rank), BF16),
            pltpu.VMEM((half, width), BF16),
            pltpu.VMEM((tok, 2 * rank), F32),
            pltpu.VMEM((n_tn, half, tn), BF16),
            dma((n_th,)),
            dma((n_tn,)),
            dma(()),
            dma(()),
            dma(()),
            dma(()),
            dma((n, CHUNKS)),
            dma(()),
            dma((n,)),
            dma(()),
            dma((n, CHUNKS)),
            dma(()),
            dma(()),
            dma(()),
            dma((n_g, n_tn)),
            dma(()),
            dma((n_g,)),
            dma(()),
            dma((n_tn,)),
            dma(()),
            dma(()),
            dma(()),
            dma(()),
            dma(()),
            dma(()),
            dma(()),
            dma(()),
            dma((n_tn, SPLIT)),
            pltpu.SMEM(routes.shape[1:], jnp.int32),
            pltpu.VMEM((2, tok), F32),
            pltpu.VMEM((rank, tok), F32),
            pltpu.VMEM((rank, width), BF16),
            pltpu.VMEM((rank, hidden_cols), BF16),
            pltpu.SMEM((examples,), jnp.int32),
            dma((6,)),
        ],
        compiler_params=pltpu.CompilerParams(
            collective_id=0, has_side_effects=True, vmem_limit_bytes=63 * 1024 * 1024
        ),
        name="window",
    )(
        cotangent[0],
        routes[0],
        gate_values[0].T,
        up_weight[0, 0],
        down_weight[0, 0],
        pre_activation[0, 0],
        input_sketch[0].T,
        model_sketch[0].T,
        hidden_sketch[0, 0].T,
        lengths[0, 0],
    )
    hand, feat = pl.pallas_call(
        functools.partial(hand_over, PARTS),
        out_shape=(
            jax.ShapeDtypeStruct(hand.shape, BF16),
            jax.ShapeDtypeStruct(feat.shape, F32),
        ),
        in_specs=[hbm, hbm],
        out_specs=(hbm, hbm),
        scratch_shapes=[
            pltpu.VMEM(hand.shape, BF16),
            pltpu.VMEM(feat.shape, F32),
            dma((PARTS + 1,)),
            dma((PARTS + 1,)),
        ],
        name="hand_over",
    )(hand, feat)
    return (hand[None], feat.reshape(1, examples, rank, 2 * rank))


def solution(mesh):
    in_specs = (
        P("section", ("groups", "dp"), None),
        P("section", ("groups", "dp"), None),
        P("section", ("groups", "dp"), None),
        P("section", "dp", None, "tensor"),
        P("section", "dp", "tensor", None),
        P("section", ("groups", "dp"), None, None, "tensor"),
        P("section", ("groups", "dp"), None),
        P("section", None, None),
        P("section", "dp", "tensor", None),
        P("section", ("groups", "dp"), None),
    )
    out_specs = (P("section", ("groups", "dp"), None), P("section", ("groups", "dp"), None, None))
    return jax.shard_map(
        per_device, mesh=mesh, in_specs=in_specs, out_specs=out_specs, check_vma=False
    )
```

```python
import functools

import jax
import jax.numpy as jnp
from jax import lax
from jax.experimental import pallas as pl
from jax.experimental.pallas import tpu as pltpu
from jax.sharding import PartitionSpec as P

EXPERTS = 4
F32 = jnp.float32
BF16 = jnp.bfloat16
NT = (((1,), (1,)), ((), ()))


def tile_of(extent, most):
    return max(t for t in range(128, most + 1, 128) if extent % t == 0)


def slots(d, n):
    upper = d // (n // 2)
    edge = d + upper * (n - 1 - 2 * d)
    side = 1 - 2 * upper
    out = [d]
    for i in range(1, n):
        near = (i + 1) // 2 if i % 2 else -(i // 2)
        both = jnp.where(2 * edge >= i, 1, 0)
        out.append(d + side * (both * near + (1 - both) * (i - edge)))
    return out


def kernel(
    n,
    sections,
    group,
    th,
    tn,
    cot_hbm,
    routes_hbm,
    gates_hbm,
    up_hbm,
    down_hbm,
    pre_hbm,
    insk_hbm,
    model_hbm,
    sketch_hbm,
    len_hbm,
    hand_out,
    feat_out,
    hand_v,
    feat_v,
    cot_all,
    wt_own,
    wt_all,
    slope_v,
    down_v2,
    up_v,
    down_v,
    pre_v,
    rows_v,
    gp_v,
    acc_v,
    mine_v,
    sk_v,
    xsend,
    xrecv,
    ssend,
    srecv,
    osend,
    orecv,
    tsend,
    trecv,
    cot_next,
    sk_sum,
    comb,
    down_sem,
    up_sem,
    pre_sem,
    own_sem,
    up_send,
    dn_send,
    ag_recv,
    wt_send,
    wt_recv,
    fw_send,
    fw_recv,
    cn_send,
    cn_recv,
    x_send,
    x_recv,
    s_send,
    s_recv,
    o_send,
    o_recv,
    t_send,
    t_recv,
    h_send,
    h_recv,
    k_send,
    k_recv,
    keep_sem,
    feat_sem,
    low_in,
    high_in,
    line_in,
    c_recv,
    routes_ref,
    gates_ref,
    insk_ref,
    model_ref,
    sketch_ref,
    len_ref,
    small_sem,
):
    tok, width = cot_hbm.shape
    half = tok // 2
    hidden_cols = up_hbm.shape[1]
    rank = insk_hbm.shape[0]
    d = lax.axis_index("dp")
    s = lax.axis_index("section")
    c = lax.axis_index("tensor")
    pc = 1 - c
    below = (s + sections - 1) % sections
    above = (s + 1) % sections
    n_groups = n // group
    n_th = hidden_cols // th
    n_tn = width // tn
    blocks = slots(d, n)
    mine_rows = pl.ds(pl.multiple_of(c * half, half), half)
    other_rows = pl.ds(pl.multiple_of(pc * half, half), half)

    def remote(src, dst, ssem, rsem, **to):
        return pltpu.make_async_remote_copy(
            src_ref=src,
            dst_ref=dst,
            send_sem=ssem,
            recv_sem=rsem,
            device_id=to,
            device_id_type=pl.DeviceIdType.MESH,
        )

    barrier = pltpu.get_barrier_semaphore()

    def signal(sem, **to):
        pl.semaphore_signal(sem, inc=1, device_id=to, device_id_type=pl.DeviceIdType.MESH)

    signal(barrier, tensor=pc)
    signal(barrier, section=below)
    if sections > 2:
        signal(barrier, section=above)
    pl.when(d > 0)(lambda: signal(barrier, dp=d - 1))
    pl.when(d < n - 1)(lambda: signal(barrier, dp=d + 1))
    sides = jnp.where(d > 0, 1, 0) + jnp.where(d < n - 1, 1, 0)
    small = [
        pltpu.make_async_copy(source, kept, small_sem.at[i])
        for i, (source, kept) in enumerate(
            (
                (routes_hbm, routes_ref),
                (gates_hbm, gates_ref),
                (sketch_hbm, sketch_ref),
                (model_hbm, model_ref),
                (insk_hbm, insk_ref),
                (len_hbm, len_ref),
            )
        )
    ]
    own_copy = pltpu.make_async_copy(cot_hbm, cot_all.at[d], own_sem)

    def pre_copy(b, i):
        return pltpu.make_async_copy(pre_hbm.at[b], pre_v.at[b], pre_sem)

    def down_copy(t):
        rows = pl.ds(pl.multiple_of(t * th, th), th)
        return pltpu.make_async_copy(down_hbm.at[rows], down_v.at[rows], down_sem.at[t])

    def up_copy(t):
        rows = pl.ds(pl.multiple_of(t * tn, tn), tn)
        return pltpu.make_async_copy(up_hbm.at[rows], up_v.at[rows], up_sem.at[t])

    for i in range(n):
        pre_copy(blocks[i], i).start()
    own_copy.start()
    for copy in small:
        copy.start()

    pl.semaphore_wait(barrier, sides + (2 if sections == 2 else 3))

    part = half // CHUNKS

    def chunk(core, j):
        return pl.ds(pl.multiple_of(core * half + j * part, part), part)

    def line_copy(b, j, to, send):
        rows = chunk(c, j)
        return remote(
            cot_all.at[b, rows], cot_all.at[b, rows], send, ag_recv.at[b, j], dp=to
        )

    def own_line(j, to, send):
        rows = chunk(c, j)
        return remote(
            cot_hbm.at[rows], cot_all.at[d, rows], send, ag_recv.at[d, j], dp=to
        )

    def up_line(b, j):
        return line_copy(b, j, jnp.minimum(d + 1, n - 1), up_send)

    def down_line(b, j):
        return line_copy(b, j, jnp.maximum(d - 1, 0), dn_send)

    def wt_copy(i, source):
        return remote(
            wt_own.at[blocks[i]], wt_all.at[source], wt_send, wt_recv.at[source], dp=blocks[i]
        )

    def fw_copy(b, j, core):
        rows = chunk(core, j)
        return remote(
            cot_all.at[b, rows], cot_all.at[b, rows], fw_send, fw_recv.at[b, j], tensor=pc
        )

    cn_copy = remote(cot_hbm.at[mine_rows], cot_next, cn_send, cn_recv, section=below)

    @pl.when(d < n - 1)
    def _():
        for j in range(CHUNKS):
            own_line(j, d + 1, up_send).start()

    @pl.when(d > 0)
    def _():
        for j in range(CHUNKS):
            own_line(j, d - 1, dn_send).start()

    cn_copy.start()
    pl.when(d == 0)(lambda: signal(low_in, dp=d + 1))
    pl.when(d == n - 1)(lambda: signal(high_in, dp=d - 1))
    pltpu.make_async_copy(pre_hbm, pre_v, pre_sem).wait()
    for t in range(n_th):
        down_copy(t).start()
    for t in range(n_tn):
        up_copy(t).start()

    @pl.when(d > 0)
    def _():
        pl.semaphore_wait(low_in, 1)
        pl.when(d < n - 1)(lambda: signal(low_in, dp=d + 1))

    @pl.when(d < n - 1)
    def _():
        pl.semaphore_wait(high_in, 1)
        pl.when(d > 0)(lambda: signal(high_in, dp=d - 1))

    for copy in small:
        copy.wait()
    block_rows = routes_ref.shape[0]
    token_block = lax.broadcasted_iota(jnp.int32, (8, tok), 1) // (tok // block_rows)
    for p in range(n):
        expert = p // (n // EXPERTS)
        weight = jnp.zeros((8, tok), F32)
        for q in range(block_rows):
            for k in range(2):
                share = jnp.where(token_block == q, gates_ref[k : k + 1, :], 0.0)
                weight += jnp.where(routes_ref[q, k] == expert, share, 0.0)
        wt_own[p] = weight

    signal(line_in, section=above)
    for i in range(1, n):
        wt_copy(i, d).start()
    own_copy.wait()

    is_upper = d >= n // 2

    def arrive(k):
        def take(b, line, may, at_once):
            def pass_chunk(j):
                pl.when(may)(lambda: line(b, j).start())

            def pass_all():
                for j in range(CHUNKS):
                    pass_chunk(j)

            for j in range(CHUNKS):
                line(b, j).wait_recv()
                pl.when(at_once)(lambda j=j: pass_chunk(j))
                fw_copy(b, j, c).start()
            pl.when(~at_once)(pass_all)

        def from_low():
            take(d - k, up_line, d < n - 1, ~is_upper | (k > 1))

        def from_high():
            take(d + k, down_line, d > 0, is_upper | (k > 1))

        pl.when(is_upper & (d >= k))(from_low)
        pl.when(d + k < n)(from_high)
        pl.when(~is_upper & (d >= k))(from_low)

    out_vec_t = lax.dot_general(
        model_ref[...], cot_all[d], NT, preferred_element_type=F32
    )
    wt_all[d] = wt_own[d]
    eye = lax.broadcasted_iota(jnp.int32, (tok, tok), 0) == lax.broadcasted_iota(
        jnp.int32, (tok, tok), 1
    )

    def x_copy(g, t):
        return remote(xsend.at[g, t], xrecv.at[g, t], x_send, x_recv.at[g, t], tensor=pc)

    def s_copy(g):
        return remote(ssend.at[g], srecv.at[g], s_send, s_recv.at[g], tensor=pc)

    def o_copy(i, t, b, source):
        return remote(
            osend.at[i, t],
            orecv.at[t, source],
            o_send,
            o_recv.at[t],
            section=below,
            dp=b,
        )

    last = n - 1
    is_end = (d == 0) | (d == n - 1)
    is_inner = (d != 0) & (d != n - 1) & ((d == 1) | (d == n - 2))
    inner = jnp.where(d == 0, 1, n - 2)

    piece = half // SPLIT

    def c_copy(t, k):
        rows = pl.ds(k * piece, piece)
        return remote(
            osend.at[last, t, rows], comb.at[t, rows], o_send, c_recv.at[t, k], dp=inner
        )

    def c_start(t):
        for k in range(SPLIT):
            c_copy(t, k).start()

    def c_onward(t, k):
        rows = pl.ds(k * piece, piece)
        b = blocks[last]
        return remote(
            osend.at[last, t, rows],
            orecv.at[t, d, rows],
            o_send,
            o_recv.at[t],
            section=below,
            dp=b,
        )

    def send_out(i, t):
        if i < last:
            o_copy(i, t, blocks[i], d).start()
            return
        pl.when(is_end)(lambda: c_start(t))
        if n > 4:
            pl.when(~is_end & ~is_inner)(lambda: o_copy(i, t, blocks[i], d).start())

    def t_copy(i, b, source):
        return remote(tsend.at[i], trecv.at[source], t_send, t_recv, dp=b)

    down_v2[...] = jnp.zeros_like(down_v2)

    def ahead(t, carry):
        rows = pl.ds(pl.multiple_of(t * th, th), th)
        sk = sketch_ref[:, rows]
        for b in range(n):
            pre = pre_v[b, :, rows].astype(F32)
            sig = jax.nn.sigmoid(pre)
            hid = (pre * sig).astype(BF16)
            slope_v[b, :, rows] = sig * (1.0 + pre * (1.0 - sig))
            down_v2[b] += lax.dot_general(hid, sk, NT, preferred_element_type=F32)
        return carry

    lax.fori_loop(0, n_th, ahead, 0)
    arrived = 0
    for g in range(n_groups):
        members = list(range(g * group, (g + 1) * group))
        while arrived < min(members[-1], n - 1):
            arrived += 1
            arrive(arrived)
        for m, i in enumerate(members):
            b = blocks[i]
            if i:
                for j in range(CHUNKS):
                    fw_copy(b, j, pc).wait_recv()
                wt_copy(i, b).wait_recv()
            row = wt_all[b][0:1, :]
            col = jnp.sum(jnp.where(eye, jnp.broadcast_to(row, (tok, tok)), 0.0), axis=1, keepdims=True)
            at = slice(m * tok, (m + 1) * tok)
            rows_v[at, :] = (col * cot_all[b].astype(F32)).astype(BF16)
            sk_v[at, :] = jnp.concatenate([down_v2[b] * col, jnp.zeros((tok, rank), F32)], axis=1)

        def first(t, carry, g=g, members=members):
            if g == 0:
                down_copy(t).wait()
            rows = pl.ds(pl.multiple_of(t * th, th), th)
            gh = lax.dot_general(rows_v[...], down_v[rows, :], NT, preferred_element_type=F32)
            for j, i in enumerate(members):
                at = slice(j * tok, (j + 1) * tok)
                gp_v[at, rows] = (gh[at] * slope_v[blocks[i], :, rows]).astype(BF16)
            return carry

        lax.fori_loop(0, n_th, first, 0)
        if arrived < n - 1:
            arrived += 1
            arrive(arrived)
        far_first = members[::-1]

        def pass_on(t, g=g, members=members, far_first=far_first):
            x_copy(g, t).wait_recv()
            cols = pl.ds(pl.multiple_of(t * tn, tn), tn)
            for i in far_first:
                j = members.index(i)
                at = slice(j * half, (j + 1) * half)
                osend[i, t] = (mine_v[at, cols] + xrecv[g, t, at, :].astype(F32)).astype(BF16)
                send_out(i, t)

        def sketch(g=g):
            sk_v[:, rank:] = lax.dot_general(
                gp_v[...], sketch_ref[...], NT, preferred_element_type=F32
            )
            for j in range(group):
                ssend[g, j * half : (j + 1) * half, :] = sk_v[
                    pl.ds(pl.multiple_of(j * tok + pc * half, half), half), :
                ]
            s_copy(g).start()

        def sketch_on(g=g, members=members):
            s_copy(g).wait_recv()
            for j, i in enumerate(members):
                at = slice(j * half, (j + 1) * half)
                total = sk_v[pl.ds(pl.multiple_of(j * tok + c * half, half), half), :] + srecv[g, at, :]
                if i:
                    tsend[i] = total.astype(BF16)
                    t_copy(i, blocks[i], d).start()
                else:
                    sk_sum[mine_rows, :] = total

        def second(t, carry, g=g, pass_on=pass_on, sketch=sketch, sketch_on=sketch_on):
            if g == 0:
                up_copy(t).wait()
            rows = pl.ds(pl.multiple_of(t * tn, tn), tn)
            acc_v[...] = lax.dot_general(gp_v[...], up_v[rows, :], NT, preferred_element_type=F32)
            for j in range(group):
                at = slice(j * half, (j + 1) * half)
                mine_v[at, rows] = acc_v[pl.ds(pl.multiple_of(j * tok + c * half, half), half), :]
                xsend[g, t, at, :] = acc_v[
                    pl.ds(pl.multiple_of(j * tok + pc * half, half), half), :
                ].astype(BF16)
            x_copy(g, t).start()

            @pl.when(t == 0)
            def _():
                sketch()
                pass_on(0)

            pl.when(t == 1)(sketch_on)

            @pl.when(t > 1)
            def _():
                pass_on(t - 1)

            return carry

        if g == 0:
            pl.semaphore_wait(line_in, 1)
        lax.fori_loop(0, n_tn, second, 0)
        need = min((g + 2) * group - 1, n - 1)
        while g + 1 < n_groups and arrived < need:
            arrived += 1
            arrive(arrived)
        if n_tn > 1:
            pass_on(n_tn - 1)

    @pl.when(is_inner)
    def _():
        for t in range(n_tn):
            for k in range(SPLIT):
                rows = slice(k * piece, (k + 1) * piece)
                c_copy(t, k).wait_recv()
                osend[last, t, rows] = (
                    osend[last, t, rows].astype(F32) + comb[t, rows].astype(F32)
                ).astype(BF16)
                c_onward(t, k).start()

    parts = pl.ds(0, n - 1)
    remote(tsend.at[parts], trecv.at[parts], t_send, t_recv, dp=blocks[1]).wait_recv()
    for i in range(1, n):
        sk_sum[mine_rows, :] += trecv[blocks[i]].astype(F32)

    def k_copy(rows):
        return remote(sk_sum.at[rows], sk_sum.at[rows], k_send, k_recv, tensor=pc)

    k_copy(mine_rows).start()
    k_copy(other_rows).wait_recv()
    sk = sk_sum[...]
    up_vec_t = sk.T[rank:, :]
    position = lax.broadcasted_iota(jnp.int32, (rank, tok), 1)
    left, right = [], []
    begin = jnp.int32(0)
    for e in range(len_ref.shape[0]):
        end = begin + len_ref[e]
        member = (position >= begin) & (position < end)
        left.append(jnp.where(member, out_vec_t, 0.0))
        right.append(jnp.where(member, up_vec_t, 0.0))
        begin = end
    exact = functools.partial(
        jnp.dot, preferred_element_type=F32, precision=lax.Precision.HIGHEST
    )
    down_feat = exact(jnp.concatenate(left, axis=0), sk[:, :rank])
    up_feat = lax.dot_general(
        jnp.concatenate(right, axis=0),
        insk_ref[...],
        NT,
        preferred_element_type=F32,
        precision=lax.Precision.HIGHEST,
    )
    feat_v[...] = jnp.concatenate([down_feat, up_feat], axis=1)
    feat_copy = pltpu.make_async_copy(feat_v, feat_out, feat_sem)
    feat_copy.start()

    cn_copy.wait_recv()
    def h_copy(t, rows):
        cols = pl.ds(t * tn, tn)
        return remote(
            hand_v.at[rows, cols], hand_out.at[rows, cols], h_send, h_recv, tensor=pc
        )

    def keep_copy(t):
        cols = pl.ds(t * tn, tn)
        return pltpu.make_async_copy(
            hand_v.at[mine_rows, cols], hand_out.at[mine_rows, cols], keep_sem
        )

    for t in range(n_tn):
        cols = slice(t * tn, (t + 1) * tn)

        def landed(count, t=t):
            box = orecv.at[t, pl.ds(0, count)]
            remote(box, box, o_send, o_recv.at[t], section=below).wait_recv()

        pl.when(is_end)(functools.partial(landed, n - 1))
        pl.when(~is_end)(functools.partial(landed, n))
        total = cot_next[:, cols].astype(F32)
        for i in range(last):
            total = total + orecv[t, blocks[i]].astype(F32)

        @pl.when(is_end)
        def _(total=total, cols=cols):
            hand_v[mine_rows, cols] = total.astype(BF16)

        @pl.when(~is_end)
        def _(total=total, cols=cols, t=t):
            hand_v[mine_rows, cols] = (total + orecv[t, blocks[last]].astype(F32)).astype(BF16)

        h_copy(t, mine_rows).start()
        keep_copy(t).start()

    remote(hand_v.at[other_rows], hand_out.at[other_rows], h_send, h_recv, tensor=pc).wait_recv()
    remote(hand_v.at[mine_rows], hand_out.at[mine_rows], h_send, h_recv, tensor=pc).wait_send()
    pltpu.make_async_copy(hand_v.at[mine_rows], hand_out.at[mine_rows], keep_sem).wait()
    feat_copy.wait()

    def drain(ref, sem):
        remote(ref, ref, sem, sem, tensor=pc).wait_send()

    drain(wt_own.at[parts], wt_send)
    drain(tsend.at[parts], t_send)
    drain(osend, o_send)
    drain(ssend, s_send)
    drain(xsend, x_send)
    drain(cot_all.at[parts, pl.ds(0, half)], fw_send)
    for m in range(1, n):
        rows = cot_all.at[pl.ds(0, m), pl.ds(0, half)]
        pl.when(d == m - 1)(functools.partial(drain, rows, up_send))
        pl.when(d == n - m)(functools.partial(drain, rows, dn_send))
    cn_copy.wait_send()
    k_copy(mine_rows).wait_send()


def hand_over(parts, hand_in, feat_in, hand_out, feat_out, hand_v, feat_v, in_sem, out_sem):
    rows = hand_in.shape[0] // parts
    into = [pltpu.make_async_copy(feat_in, feat_v, in_sem.at[parts])]
    out = [pltpu.make_async_copy(feat_v, feat_out, out_sem.at[parts])]
    for j in range(parts):
        at = pl.ds(j * rows, rows)
        into.append(pltpu.make_async_copy(hand_in.at[at], hand_v.at[at], in_sem.at[j]))
        out.append(pltpu.make_async_copy(hand_v.at[at], hand_out.at[at], out_sem.at[j]))
    for copy in into:
        copy.start()
    for copy, then in zip(into, out):
        copy.wait()
        then.start()
    for copy in out:
        copy.wait()


GROUP = 2
SPLIT = 1
PARTS = 1
CHUNKS = 2


def per_device(
    cotangent,
    routes,
    gate_values,
    up_weight,
    down_weight,
    pre_activation,
    input_sketch,
    model_sketch,
    hidden_sketch,
    lengths,
):
    n = lax.axis_size("dp")
    sections = lax.axis_size("section")
    tok, width = cotangent.shape[1:]
    rank = model_sketch.shape[2]
    hidden_cols = up_weight.shape[3]
    examples = lengths.shape[2]
    group = GROUP
    half = tok // 2
    m = group * tok
    th = tile_of(hidden_cols, 896)
    tn = tile_of(width, 512)
    n_th, n_tn, n_g = hidden_cols // th, width // tn, n // group
    dma = pltpu.SemaphoreType.DMA
    hbm = pl.BlockSpec(memory_space=pl.ANY)
    hand, feat = pl.pallas_call(
        functools.partial(kernel, n, sections, group, th, tn),
        out_shape=(
            jax.ShapeDtypeStruct((tok, width), BF16),
            jax.ShapeDtypeStruct((examples * rank, 2 * rank), F32),
        ),
        in_specs=[hbm] * 10,
        out_specs=(hbm, hbm),
        scratch_shapes=[
            pltpu.VMEM((tok, width), BF16),
            pltpu.VMEM((examples * rank, 2 * rank), F32),
            pltpu.VMEM((n, tok, width), BF16),
            pltpu.VMEM((n, 8, tok), F32),
            pltpu.VMEM((n, 8, tok), F32),
            pltpu.VMEM((n, tok, hidden_cols), F32),
            pltpu.VMEM((n, tok, rank), F32),
            pltpu.VMEM((width, hidden_cols), BF16),
            pltpu.VMEM((hidden_cols, width), BF16),
            pltpu.VMEM((n, tok, hidden_cols), BF16),
            pltpu.VMEM((m, width), BF16),
            pltpu.VMEM((m, hidden_cols), BF16),
            pltpu.VMEM((m, tn), F32),
            pltpu.VMEM((m // 2, width), F32),
            pltpu.VMEM((m, 2 * rank), F32),
            pltpu.VMEM((n_g, n_tn, m // 2, tn), BF16),
            pltpu.VMEM((n_g, n_tn, m // 2, tn), BF16),
            pltpu.VMEM((n_g, m // 2, 2 * rank), F32),
            pltpu.VMEM((n_g, m // 2, 2 * rank), F32),
            pltpu.VMEM((n, n_tn, half, tn), BF16),
            pltpu.VMEM((n_tn, n, half, tn), BF16),
            pltpu.VMEM((n, half, 2 * rank), BF16),
            pltpu.VMEM((n, half, 2 * rank), BF16),
            pltpu.VMEM((half, width), BF16),
            pltpu.VMEM((tok, 2 * rank), F32),
            pltpu.VMEM((n_tn, half, tn), BF16),
            dma((n_th,)),
            dma((n_tn,)),
            dma(()),
            dma(()),
            dma(()),
            dma(()),
            dma((n, CHUNKS)),
            dma(()),
            dma((n,)),
            dma(()),
            dma((n, CHUNKS)),
            dma(()),
            dma(()),
            dma(()),
            dma((n_g, n_tn)),
            dma(()),
            dma((n_g,)),
            dma(()),
            dma((n_tn,)),
            dma(()),
            dma(()),
            dma(()),
            dma(()),
            dma(()),
            dma(()),
            dma(()),
            dma(()),
            pltpu.SemaphoreType.REGULAR,
            pltpu.SemaphoreType.REGULAR,
            pltpu.SemaphoreType.REGULAR,
            dma((n_tn, SPLIT)),
            pltpu.SMEM(routes.shape[1:], jnp.int32),
            pltpu.VMEM((2, tok), F32),
            pltpu.VMEM((rank, tok), F32),
            pltpu.VMEM((rank, width), BF16),
            pltpu.VMEM((rank, hidden_cols), BF16),
            pltpu.SMEM((examples,), jnp.int32),
            dma((6,)),
        ],
        compiler_params=pltpu.CompilerParams(
            collective_id=0, has_side_effects=True, vmem_limit_bytes=63 * 1024 * 1024
        ),
        name="window",
    )(
        cotangent[0],
        routes[0],
        gate_values[0].T,
        up_weight[0, 0],
        down_weight[0, 0],
        pre_activation[0, 0],
        input_sketch[0].T,
        model_sketch[0].T,
        hidden_sketch[0, 0].T,
        lengths[0, 0],
    )
    hand, feat = pl.pallas_call(
        functools.partial(hand_over, PARTS),
        out_shape=(
            jax.ShapeDtypeStruct(hand.shape, BF16),
            jax.ShapeDtypeStruct(feat.shape, F32),
        ),
        in_specs=[hbm, hbm],
        out_specs=(hbm, hbm),
        scratch_shapes=[
            pltpu.VMEM(hand.shape, BF16),
            pltpu.VMEM(feat.shape, F32),
            dma((PARTS + 1,)),
            dma((PARTS + 1,)),
        ],
        name="hand_over",
    )(hand, feat)
    return (hand[None], feat.reshape(1, examples, rank, 2 * rank))


def solution(mesh):
    in_specs = (
        P("section", ("groups", "dp"), None),
        P("section", ("groups", "dp"), None),
        P("section", ("groups", "dp"), None),
        P("section", "dp", None, "tensor"),
        P("section", "dp", "tensor", None),
        P("section", ("groups", "dp"), None, None, "tensor"),
        P("section", ("groups", "dp"), None),
        P("section", None, None),
        P("section", "dp", "tensor", None),
        P("section", ("groups", "dp"), None),
    )
    out_specs = (P("section", ("groups", "dp"), None), P("section", ("groups", "dp"), None, None))
    return jax.shard_map(
        per_device, mesh=mesh, in_specs=in_specs, out_specs=out_specs, check_vma=False
    )
```
